512 devices in a mesh: dp: 16 (over y, z_lo), seq: 32 (over z_hi, x, core).
Axes of the slice: x: 4, y: 4, z: 16 (z_hi: 4, z_lo: 4; z = z_hi * 4 + z_lo), core: 2. Of those that a mesh axis runs over, the one named last changes fastest.
Arguments:
- residual_stream: bfloat16 [65536, 512], P(('dp', 'seq')), parts along dimension 0, may hold values from -6 to 6
- norm_gain: float32 [512], replicated, may hold values from 0.5 to 1.5
- in_proj: bfloat16 [512, 2048], replicated, may hold values from -0.25 to 0.25
- conv_weight: float32 [4, 1024], replicated, may hold values from -3 to 3
- conv_bias: float32 [1024], replicated, may hold values from -0.5 to 0.5
- state_proj: bfloat16 [1024, 64], replicated, may hold values from -0.1875 to 0.1875
- step_proj: bfloat16 [32, 1024], replicated, may hold values from -1 to 1
- step_bias: float32 [1024], replicated, may hold values from -4 to 0
- decay_rate: float32 [1024, 16], replicated, may hold values from 0.0001 to 1
- skip_gain: float32 [1024], replicated, may hold values from 0.5 to 1.5
- out_proj: bfloat16 [1024, 512], replicated, may hold values from -0.1875 to 0.1875
Outputs:
- block_out: bfloat16 [65536, 512], P(('dp', 'seq')), parts along dimension 0
The draws below stay inside these ranges and needn't reach their ends.
There are 16 independent parts, one for each index of `dp`. The reference program is written for one: setup_inputs(seed, part) draws one part's arguments, and reference() takes and returns one part's arrays. A program takes and returns all parts, laid end to end along the dimension named above; an argument that names none is the same for every part. Nothing has to cross between parts.
All inputs are finite; a program needn't handle non-finite values.
Results may differ from the reference program's by a relative error of at most 0.012.
Values may be sent and summed in bfloat16 or wider, within the bound.
A program may use at most 64 MiB of HBM per device.

```python
import math
import jax
import jax.numpy as jnp
from jax import lax

D = 512
E = 1024
N = 16
R = 32
K = 4
TOK_DEV = 128
L = 4096


def draw_residual_stream(key, part):
    blocks = L // TOK_DEV
    jitter_key = jax.random.fold_in(key, 11)
    heading_key = jax.random.fold_in(key, 23)
    strength_key = jax.random.fold_in(key, 37)
    jitter = 0.4 * jax.random.normal(jitter_key, (blocks, TOK_DEV, D), jnp.float32)
    heading = jax.random.normal(heading_key, (blocks, 1, D), jnp.float32)
    strength = jnp.exp(jax.random.uniform(strength_key, (blocks, 1, 1), jnp.float32, math.log(0.5), math.log(1.5)))
    values = jnp.clip(jitter + strength * heading, -6.0, 6.0)
    return values.reshape(L, D).astype(jnp.bfloat16)


def scatter_about(key, extent, scale, reach, kind=jnp.bfloat16):
    entries = scale * jax.random.normal(key, extent, jnp.float32)
    return jnp.clip(entries, min=-reach, max=reach).astype(kind)


def setup_inputs(seed: int = 0, part: int = 0) -> dict:
    splits = jax.random.split(jax.random.key(seed), 12)
    part_keys = jax.random.split(jax.random.fold_in(splits[11], part), 12)
    residual_stream = draw_residual_stream(jax.random.fold_in(jax.random.fold_in(splits[11], part), 71), part)
    norm_gain = jnp.clip(1.0 + 0.1 * jax.random.normal(splits[1], (D,), jnp.float32), 0.5, 1.5)
    in_proj = scatter_about(splits[2], (D, 2 * E), D ** -0.5, 0.25)
    conv_weight = scatter_about(splits[3], (K, E), K ** -0.5, 3.0, jnp.float32)
    conv_bias = jnp.clip(jax.random.uniform(splits[4], (E,), jnp.float32, -0.5, 0.5), -0.5, 0.5)
    state_proj = scatter_about(splits[5], (E, R + 2 * N), E ** -0.5, 0.1875)
    step_proj = scatter_about(splits[6], (R, E), R ** -0.5, 1.0)
    step_bias = jnp.clip(jax.random.uniform(splits[7], (E,), jnp.float32, -4.0, 0.0), -4.0, 0.0)
    decay_rate = jnp.clip(jnp.exp(jax.random.uniform(splits[8], (E, N), jnp.float32, math.log(0.0001), math.log(1.0))), 0.0001, 1.0)
    skip_gain = jnp.clip(jax.random.uniform(splits[9], (E,), jnp.float32, 0.5, 1.5), 0.5, 1.5)
    out_proj = scatter_about(splits[10], (E, D), E ** -0.5, 0.1875)
    return {"residual_stream": residual_stream, "norm_gain": norm_gain, "in_proj": in_proj, "conv_weight": conv_weight, "conv_bias": conv_bias, "state_proj": state_proj, "step_proj": step_proj, "step_bias": step_bias, "decay_rate": decay_rate, "skip_gain": skip_gain, "out_proj": out_proj}


def normalize(values, norm_gain):
    inv_scale = lax.rsqrt(lax.optimization_barrier(jnp.mean(values * values, axis=-1, keepdims=True)) + 1e-05)
    return (values * inv_scale * norm_gain).astype(jnp.bfloat16)

def mixer(normed, in_proj, conv_weight, conv_bias, state_proj, step_proj, step_bias, decay_rate, skip_gain, out_proj):
    length = normed.shape[0]
    joined = jnp.dot(normed, in_proj, preferred_element_type=jnp.float32).astype(jnp.bfloat16)
    inner_part = joined[:, :E].astype(jnp.float32)
    gate_part = joined[:, E:].astype(jnp.float32)
    padded = jnp.concatenate([jnp.zeros((K - 1, E), jnp.float32), inner_part], axis=0)
    conv_sum = conv_bias[None, :] + jnp.zeros((length, E), jnp.float32)
    for offset in range(K):
        conv_sum = conv_sum + conv_weight[offset][None, :] * padded[offset:offset + length]
    activated = jax.nn.silu(conv_sum).astype(jnp.bfloat16)
    projected = jnp.dot(activated, state_proj, preferred_element_type=jnp.float32)
    step_low = projected[:, :R].astype(jnp.bfloat16)
    input_map = projected[:, R:R + N]
    output_map = projected[:, R + N:]
    step_size = jax.nn.softplus(jnp.dot(step_low, step_proj, preferred_element_type=jnp.float32) + step_bias)
    signal = activated.astype(jnp.float32)

    def advance(carried, inputs):
        step_row, signal_row, input_row, output_row = inputs
        carried = jnp.exp(-step_row[:, None] * decay_rate) * carried + (step_row * signal_row)[:, None] * input_row[None, :]
        return (carried, lax.optimization_barrier(jnp.sum(carried * output_row[None, :], axis=1)))
    _, scanned = lax.scan(advance, jnp.zeros((E, N), jnp.float32), (step_size, signal, input_map, output_map))
    gated_mix = (scanned + skip_gain * signal) * jax.nn.silu(gate_part)
    return jnp.dot(gated_mix.astype(jnp.bfloat16), out_proj, preferred_element_type=jnp.float32).astype(jnp.bfloat16)

def reference(residual_stream, norm_gain, in_proj, conv_weight, conv_bias, state_proj, step_proj, step_bias, decay_rate, skip_gain, out_proj):
    hidden = residual_stream.astype(jnp.float32)
    forward = mixer(normalize(hidden, norm_gain), in_proj, conv_weight, conv_bias, state_proj, step_proj, step_bias, decay_rate, skip_gain, out_proj)
    flipped = hidden[::-1, ::-1]
    mirrored = mixer(normalize(flipped, norm_gain), in_proj, conv_weight, conv_bias, state_proj, step_proj, step_bias, decay_rate, skip_gain, out_proj)
    summed = hidden + forward.astype(jnp.float32) + mirrored.astype(jnp.float32)[::-1, ::-1]
    return summed.astype(jnp.bfloat16)
```

```python
import functools
import math

import jax
import jax.numpy as jnp
from jax import lax
from jax.experimental import pallas as pl
from jax.experimental.pallas import tpu as pltpu
from jax.sharding import PartitionSpec as P

F32 = jnp.float32
BF16 = jnp.bfloat16
LOG2E = math.log2(math.e)
GROUP = 8
FAR = 4
LANES = 128
ROWS = 8


def dot(a, b):
    return jnp.dot(a, b, preferred_element_type=F32)


def split2(v):
    high = v.astype(BF16)
    return high, (v - high.astype(F32)).astype(BF16)


def anti_identity():
    row = lax.broadcasted_iota(jnp.int32, (LANES, LANES), 0)
    col = lax.broadcasted_iota(jnp.int32, (LANES, LANES), 1)
    return (row + col == LANES - 1).astype(F32).astype(BF16)


def flip_lanes(v, anti):
    pieces = [v[:, i : i + LANES] for i in range(0, v.shape[1], LANES)]
    return jnp.concatenate([dot(p, anti) for p in pieces[::-1]], axis=1)


def inv_rms(v):
    return lax.rsqrt(jnp.mean(v * v, axis=-1, keepdims=True) + 1e-05)


def softplus(v):
    return jnp.maximum(v, 0.0) + jnp.log1p(jnp.exp(-jnp.abs(v)))


def silu(v):
    return v * jax.nn.sigmoid(v)


def kernel(
    x_ref, gain_ref, in_ref, cw_ref, cb_ref, sp_ref, tp_ref, tb_ref, decay_ref, skip_ref, out_ref,
    o_ref,
    halo, nrm, a2, edge, u_s, proj, proj_t, dt_s, du_s, hist, cblk, cum, gc, pre, sg, gmix,
    send_a, recv_a, send_z, recv_z, send_c, recv_c, hin,
    halo_send, halo_recv, a_send, a_recv, z_send, z_recv, c_send, c_recv,
):
    tokens, width = x_ref.shape
    inner_width = cw_ref.shape[1]
    taps = cw_ref.shape[0]
    rank = tp_ref.shape[0]
    states = decay_ref.shape[1]
    blocks = tokens // ROWS
    slices = inner_width // LANES
    index = lax.axis_index("seq")
    count = GROUP * FAR
    far = index // GROUP
    place = index % GROUP
    left = (index + count - 1) % count
    right = (index + 1) % count
    members = [far * GROUP + (place + d) % GROUP for d in range(1, GROUP)]
    distant = [((far + d) % FAR) * GROUP + place for d in range(1, FAR)]

    barrier = pltpu.get_barrier_semaphore()
    for peer in [left, right] + members + distant:
        pl.semaphore_signal(
            barrier, inc=1, device_id={"seq": peer}, device_id_type=pl.DeviceIdType.MESH
        )

    def remote(src, dst, send, recv, peer):
        return pltpu.make_async_remote_copy(
            src_ref=src, dst_ref=dst, send_sem=send, recv_sem=recv,
            device_id={"seq": peer}, device_id_type=pl.DeviceIdType.MESH,
        )

    row = lax.broadcasted_iota(jnp.int32, (states, states), 0)
    col = lax.broadcasted_iota(jnp.int32, (states, states), 1)
    unit = (row == col).astype(F32).astype(BF16)
    rates = decay_ref[...]
    p1 = rates.astype(BF16)
    rest = rates - p1.astype(F32)
    p2 = rest.astype(BF16)
    p3 = (rest - p2.astype(F32)).astype(BF16)
    across = (((1,), (1,)), ((), ()))
    turned = sum(
        lax.dot_general(unit, p, across, preferred_element_type=F32) for p in (p1, p2, p3)
    )
    turned = turned * (-LOG2E)
    for k in range(slices):
        a2[k] = turned[:, k * LANES : (k + 1) * LANES]

    def a2_wide(first=0, last=slices):
        return jnp.concatenate([a2[k] for k in range(first, last)], axis=1)

    anti = anti_identity()
    gain = gain_ref[...]
    x = x_ref[...]
    x32 = x.astype(F32)
    scale = inv_rms(x32)
    nrm[0] = (x32 * scale * gain).astype(BF16)
    nrm[1] = (flip_lanes(x, anti) * scale * gain).astype(BF16)

    def convolve(v, branch, cols):
        total = cb_ref[:, cols]
        size = v.shape[0]
        for k in range(taps):
            back = taps - 1 - k
            shift = back if branch == 0 else (size - back) % size
            moved = v if back == 0 else pltpu.roll(v, shift, 0)
            total = total + cw_ref[k : k + 1, cols] * moved
        return silu(total).astype(BF16)

    wide = 256

    def front(i, _):
        cols = pl.ds(pl.multiple_of(i * wide, wide), wide)
        for branch in range(2):
            inner = dot(nrm[branch], in_ref[:, cols])
            edge[branch, :, cols] = inner[:ROWS] if branch == 0 else inner[tokens - ROWS :]
            u_s[branch, :, cols] = convolve(inner, branch, cols).astype(F32)
        return 0

    lax.fori_loop(0, inner_width // wide, front, 0)

    for branch in range(2):
        proj[branch] = dot(u_s[branch].astype(BF16), sp_ref[...])

    def steps(i, _):
        cols = pl.ds(pl.multiple_of(i * wide, wide), wide)
        for branch in range(2):
            low = proj[branch, :, :rank].astype(BF16)
            dt = softplus(dot(low, tp_ref[:, cols]) + tb_ref[:, cols])
            dt_s[branch, :, cols] = dt
            du_s[branch, :, cols] = dt * u_s[branch, :, cols]
        return 0

    lax.fori_loop(0, inner_width // wide, steps, 0)

    pl.semaphore_wait(barrier, 2 + len(members) + len(distant))
    edge_rows = halo.shape[1]
    to_right = remote(
        x_ref.at[pl.ds(tokens - edge_rows, edge_rows)], halo.at[0], halo_send.at[0], halo_recv.at[0], right
    )
    to_left = remote(x_ref.at[pl.ds(0, edge_rows)], halo.at[1], halo_send.at[1], halo_recv.at[1], left)
    to_right.start()
    to_left.start()

    def turn_proj():
        proj_t[...] = jnp.concatenate([proj[0], proj[1]], axis=1).T

    proj_width = proj.shape[2]
    turn_proj()
    half = slices // 2

    def scan(first, last):
        ends = []
        for part in range(2):
            lanes = pl.ds(part * half * LANES, half * LANES)
            rate = a2_wide(part * half, (part + 1) * half)

            def chunk(c, carried, lanes=lanes, rate=rate):
                carried = list(carried)
                base = c * ROWS
                rolled = [
                    pltpu.roll(proj_t[rank : rank + states, :], (tokens - base) % tokens, 1),
                    pltpu.roll(
                        proj_t[proj_width + rank : proj_width + rank + states, :],
                        (base + ROWS) % tokens, 1,
                    ),
                ]
                for j in range(ROWS):
                    for branch in range(2):
                        t = base + j if branch == 0 else tokens - 1 - base - j
                        pick = j if branch == 0 else ROWS - 1 - j
                        column = jnp.broadcast_to(rolled[branch][:, pick : pick + 1], (states, LANES))
                        column = jnp.concatenate([column] * half, axis=1)
                        dt = jnp.broadcast_to(dt_s[branch, pl.ds(t, 1), lanes], (states, half * LANES))
                        du = jnp.broadcast_to(du_s[branch, pl.ds(t, 1), lanes], (states, half * LANES))
                        h = jnp.exp2(dt * rate) * carried[branch] + du * column
                        hist[branch, pl.ds(pl.multiple_of(t * states, states), states), lanes] = h.astype(BF16)
                        carried[branch] = h
                return tuple(carried)

            zero = jnp.zeros((states, half * LANES), F32)
            ends.append(lax.fori_loop(first, last, chunk, (zero, zero)))
        return ends

    main = scan(1, blocks)
    for part in range(2):
        for branch in range(2):
            for k in range(half):
                hin[branch, part * half + k] = main[part][branch][:, k * LANES : (k + 1) * LANES]

    to_right.wait()
    to_left.wait()
    border = halo[...]
    near = border[0].astype(F32)
    far_side = border[1]
    far32 = far_side.astype(F32)
    ahead = (near * inv_rms(near) * gain).astype(BF16)
    behind = (flip_lanes(far_side, anti) * inv_rms(far32) * gain).astype(BF16)
    has_left = (index > 0).astype(F32)
    has_right = (index < count - 1).astype(F32)

    def border_front(i, _):
        cols = pl.ds(pl.multiple_of(i * wide, wide), wide)
        weights = in_ref[:, cols]
        v = dot(ahead, weights)[edge_rows - ROWS :] * has_left
        joined = jnp.concatenate([v, edge[0, :, cols]], axis=0)
        u_s[0, 0:ROWS, cols] = convolve(joined, 0, cols).astype(F32)[ROWS:]
        v = dot(behind, weights)[:ROWS] * has_right
        joined = jnp.concatenate([edge[1, :, cols], v], axis=0)
        u_s[1, tokens - ROWS : tokens, cols] = convolve(joined, 1, cols).astype(F32)[:ROWS]
        return 0

    lax.fori_loop(0, inner_width // wide, border_front, 0)
    border_u = jnp.concatenate([u_s[0, 0:ROWS], u_s[1, tokens - ROWS : tokens]], axis=0)
    border_p = dot(border_u.astype(BF16), sp_ref[...])
    proj[0, 0:ROWS] = border_p[:ROWS]
    proj[1, tokens - ROWS : tokens] = border_p[ROWS:]
    border_dt = softplus(dot(border_p[:, :rank].astype(BF16), tp_ref[...]) + tb_ref[...])
    border_du = border_dt * border_u
    dt_s[0, 0:ROWS] = border_dt[:ROWS]
    dt_s[1, tokens - ROWS : tokens] = border_dt[ROWS:]
    du_s[0, 0:ROWS] = border_du[:ROWS]
    du_s[1, tokens - ROWS : tokens] = border_du[ROWS:]
    turn_proj()
    start = scan(0, 1)

    def wide_tile(rows):
        return jnp.concatenate(rows + [jnp.zeros((16 - len(rows), LANES), F32)], axis=0)

    main_tot = [
        jnp.sum(dt_s[0, ROWS:tokens], axis=0, keepdims=True),
        jnp.sum(dt_s[1, 0 : tokens - ROWS], axis=0, keepdims=True),
    ]
    start_tot = [
        jnp.sum(border_dt[:ROWS], axis=0, keepdims=True),
        jnp.sum(border_dt[ROWS:], axis=0, keepdims=True),
    ]

    def tot_rows(values):
        rows = []
        for v in values:
            high = v.astype(BF16).astype(F32)
            rows += [high, v - high]
        return wide_tile(rows).astype(BF16)

    for k in range(slices):
        lanes = slice(k * LANES, (k + 1) * LANES)
        part, inside = divmod(k, half)
        own = slice(inside * LANES, (inside + 1) * LANES)
        for branch in range(2):
            first = start[part][branch][:, own]
            grown = jnp.exp2(main_tot[branch][:, lanes] * a2[k]) * first + hin[branch, k]
            send_a[k, branch] = grown.astype(BF16)
            hist_keep = first
            hin[branch, k] = hist_keep
        send_a[k, 2] = tot_rows([(main_tot[b] + start_tot[b])[:, lanes] for b in range(2)])

    copies_a = []
    for d, peer in enumerate(members):
        target = (place + d + 1) % GROUP
        copies_a.append(
            remote(send_a.at[target], recv_a.at[place], a_send.at[d], a_recv.at[d], peer)
        )
    for c in copies_a:
        c.start()
    recv_a[place] = send_a[place]
    recv_z[far] = jnp.zeros(recv_z.shape[1:], BF16)

    def gates(i, _):
        cols = pl.ds(pl.multiple_of(i * wide, wide), wide)
        behind_cols = pl.ds(pl.multiple_of(inner_width + i * wide, wide), wide)
        for branch in range(2):
            sg[branch, :, cols] = silu(dot(nrm[branch], in_ref[:, behind_cols]))
        return 0

    lax.fori_loop(0, inner_width // wide, gates, 0)

    for c in copies_a:
        c.wait()

    rate = a2[place]
    got_s = [[recv_a[m, b].astype(F32) for m in range(GROUP)] for b in range(2)]
    got_t = []
    for m in range(GROUP):
        rows = recv_a[m, 2].astype(F32)
        got_t.append([rows[0:1] + rows[1:2], rows[2:3] + rows[3:4]])

    prefix = [[None] * GROUP, [None] * GROUP]
    before = [[None] * GROUP, [None] * GROUP]
    for branch in range(2):
        state = jnp.zeros((states, LANES), F32)
        total = jnp.zeros((1, LANES), F32)
        order = range(GROUP) if branch == 0 else range(GROUP - 1, -1, -1)
        for m in order:
            prefix[branch][m] = state
            before[branch][m] = total
            state = jnp.exp2(got_t[m][branch] * rate) * state + got_s[branch][m]
            total = total + got_t[m][branch]
        send_z[branch, 0] = state.astype(BF16)
        send_z[branch, 1] = tot_rows([total])

    copies_z = []
    for d, peer in enumerate(distant):
        target = (far + d + 1) % FAR
        branch = (target < far).astype(jnp.int32)
        copies_z.append(
            remote(send_z.at[branch], recv_z.at[far], z_send.at[d], z_recv.at[d], peer)
        )
    for c in copies_z:
        c.start()

    t_row = lax.broadcasted_iota(jnp.int32, (tokens, tokens), 0)
    t_col = lax.broadcasted_iota(jnp.int32, (tokens, tokens), 1)
    below = [
        (t_col <= t_row) & ((t_col < ROWS) == (t_row < ROWS)),
        (t_col >= t_row) & ((t_col >= tokens - ROWS) == (t_row >= tokens - ROWS)),
    ]
    for branch in range(2):
        ones = below[branch].astype(F32).astype(BF16)
        high, low = split2(dt_s[branch])
        cum[branch] = dot(ones, high) + dot(ones, low)

    c_first = rank + states
    pick_row = lax.broadcasted_iota(jnp.int32, (states, 256), 0)
    pick_col = lax.broadcasted_iota(jnp.int32, (states, 256), 1)
    spread = (pick_col % states == pick_row).astype(F32).astype(BF16)
    own_row = lax.broadcasted_iota(jnp.int32, (tokens, 256), 0)
    own_col = lax.broadcasted_iota(jnp.int32, (tokens, 256), 1)
    own = own_col // states == own_row % (256 // states)
    for branch in range(2):
        maps = proj[branch, :, c_first : c_first + states].astype(BF16)
        cblk[branch] = jnp.where(own, dot(maps, spread), 0.0).astype(BF16)

    run = 256 // states

    def local_out(i, _):
        rows = pl.ds(pl.multiple_of(i * run, run), run)
        deep = pl.ds(pl.multiple_of(i * 256, 256), 256)
        for branch in range(2):
            local = dot(cblk[branch, rows, :], hist[branch, deep, :])
            pre[branch, rows, :] = local + skip_ref[...] * u_s[branch, rows, :]
        return 0

    lax.fori_loop(0, tokens // run, local_out, 0)

    def factors(i, _):
        rows = pl.ds(pl.multiple_of(i * ROWS, ROWS), ROWS)
        for branch in range(2):
            maps = proj[branch, rows, :]
            for n in range(states):
                c_col = jnp.broadcast_to(maps[:, c_first + n : c_first + n + 1], (ROWS, LANES))
                for k in range(slices):
                    seen = cum[branch, rows, k * LANES : (k + 1) * LANES]
                    gc[branch, k, n, rows, :] = jnp.exp2(seen * a2[k, n : n + 1, :]) * c_col
        return 0

    lax.fori_loop(0, blocks, factors, 0)

    for c in copies_z:
        c.wait()

    for branch in range(2):
        state = jnp.zeros((states, LANES), F32)
        order = range(FAR) if branch == 0 else range(FAR - 1, -1, -1)
        for z in order:
            here = (z < far) if branch == 0 else (z > far)
            rows = recv_z[z, 1].astype(F32)
            later = jnp.exp2((rows[0:1] + rows[1:2]) * rate) * state + recv_z[z, 0].astype(F32)
            state = jnp.where(here, later, state)
        for m in range(GROUP):
            entering = jnp.exp2(before[branch][m] * rate) * state + prefix[branch][m]
            send_c[m, branch] = entering.astype(BF16)

    copies_c = []
    for d, peer in enumerate(members):
        target = (place + d + 1) % GROUP
        copies_c.append(
            remote(send_c.at[target], recv_c.at[place], c_send.at[d], c_recv.at[d], peer)
        )
    for c in copies_c:
        c.start()
    recv_c[place] = send_c[place]
    for c in copies_c:
        c.wait()

    for branch in range(2):
        for k in range(slices):
            entering = recv_c[k, branch].astype(F32)
            gone = jnp.exp2(start_tot[branch][:, k * LANES : (k + 1) * LANES] * a2[k])
            hin[branch, k] = gone * entering + hin[branch, k]

    def finish(k, _):
        cols = pl.ds(pl.multiple_of(k * LANES, LANES), LANES)
        for branch in range(2):
            spread_h = [
                jnp.broadcast_to(hin[branch, k, n : n + 1, :], (ROWS, LANES)) for n in range(states)
            ]
            edge_h = recv_c[k, branch].astype(F32)
            border_block = 0 if branch == 0 else blocks - 1
            pieces = []
            for b in range(blocks):
                rows = slice(b * ROWS, (b + 1) * ROWS)
                total = pre[branch, rows, cols]
                for n in range(states):
                    if b == border_block:
                        h = jnp.broadcast_to(edge_h[n : n + 1, :], (ROWS, LANES))
                    else:
                        h = spread_h[n]
                    total = total + gc[branch, k, n, rows, :] * h
                pieces.append(total * sg[branch, rows, cols])
                if len(pieces) == 2:
                    gmix[branch, (b - 1) * ROWS : (b + 1) * ROWS, cols] = jnp.concatenate(
                        pieces, axis=0
                    ).astype(BF16)
                    pieces = []
        return 0

    lax.fori_loop(0, slices, finish, 0)
    forward = dot(gmix[0], out_ref[...]).astype(BF16)
    flipped = flip_lanes(dot(gmix[1], out_ref[...]).astype(BF16), anti)
    o_ref[...] = (x_ref[...].astype(F32) + forward.astype(F32) + flipped).astype(BF16)


def shards(
    residual_stream, norm_gain, in_proj, conv_weight, conv_bias, state_proj, step_proj,
    step_bias, decay_rate, skip_gain, out_proj,
):
    tokens, width = residual_stream.shape
    inner_width = conv_weight.shape[1]
    states = decay_rate.shape[1]
    slices = inner_width // LANES
    vmem = pl.BlockSpec(memory_space=pltpu.VMEM)
    by_token = (2, tokens, inner_width)
    scratch = [
        pltpu.VMEM((2, 16, width), BF16),
        pltpu.VMEM((2, tokens, width), BF16),
        pltpu.VMEM((slices, states, LANES), F32),
        pltpu.VMEM((2, ROWS, inner_width), F32),
        pltpu.VMEM(by_token, F32),
        pltpu.VMEM((2, tokens, state_proj.shape[1]), F32),
        pltpu.VMEM((2 * state_proj.shape[1], tokens), F32),
        pltpu.VMEM(by_token, F32),
        pltpu.VMEM(by_token, F32),
        pltpu.VMEM((2, tokens * states, inner_width), BF16),
        pltpu.VMEM((2, tokens, 256), BF16),
        pltpu.VMEM(by_token, F32),
        pltpu.VMEM((2, slices, states, tokens, LANES), F32),
        pltpu.VMEM(by_token, F32),
        pltpu.VMEM(by_token, F32),
        pltpu.VMEM(by_token, BF16),
        pltpu.VMEM((GROUP, 3, states, LANES), BF16),
        pltpu.VMEM((GROUP, 3, states, LANES), BF16),
        pltpu.VMEM((2, 2, states, LANES), BF16),
        pltpu.VMEM((FAR, 2, states, LANES), BF16),
        pltpu.VMEM((GROUP, 2, states, LANES), BF16),
        pltpu.VMEM((GROUP, 2, states, LANES), BF16),
        pltpu.VMEM((2, slices, states, LANES), F32),
        pltpu.SemaphoreType.DMA((2,)),
        pltpu.SemaphoreType.DMA((2,)),
        pltpu.SemaphoreType.DMA((GROUP - 1,)),
        pltpu.SemaphoreType.DMA((GROUP - 1,)),
        pltpu.SemaphoreType.DMA((FAR - 1,)),
        pltpu.SemaphoreType.DMA((FAR - 1,)),
        pltpu.SemaphoreType.DMA((GROUP - 1,)),
        pltpu.SemaphoreType.DMA((GROUP - 1,)),
    ]
    return pl.pallas_call(
        kernel,
        out_shape=jax.ShapeDtypeStruct((tokens, width), BF16),
        in_specs=[vmem] * 11,
        out_specs=vmem,
        scratch_shapes=scratch,
        compiler_params=pltpu.CompilerParams(
            collective_id=0, has_side_effects=True, vmem_limit_bytes=60 << 20
        ),
    )(
        residual_stream,
        norm_gain.reshape(1, -1),
        in_proj,
        conv_weight,
        conv_bias.reshape(1, -1),
        state_proj,
        step_proj,
        step_bias.reshape(1, -1),
        decay_rate,
        skip_gain.reshape(1, -1),
        out_proj,
    )


def solution(mesh):
    return jax.shard_map(
        shards,
        mesh=mesh,
        in_specs=(P(("dp", "seq"), None), P(), P(), P(), P(), P(), P(), P(), P(), P(), P()),
        out_specs=P(("dp", "seq"), None),
        check_vma=False,
    )
```

```python
import functools
import math

import jax
import jax.numpy as jnp
from jax import lax
from jax.experimental import pallas as pl
from jax.experimental.pallas import tpu as pltpu
from jax.sharding import PartitionSpec as P

F32 = jnp.float32
BF16 = jnp.bfloat16
LOG2E = math.log2(math.e)
GROUP = 8
FAR = 4
LANES = 128
ROWS = 8


def dot(a, b):
    return jnp.dot(a, b, preferred_element_type=F32)


def dot_nt(a, b):
    return lax.dot_general(a, b, (((1,), (1,)), ((), ())), preferred_element_type=F32)


def split2(v):
    high = v.astype(BF16)
    return high, (v - high.astype(F32)).astype(BF16)


def anti_identity():
    row = lax.broadcasted_iota(jnp.int32, (LANES, LANES), 0)
    col = lax.broadcasted_iota(jnp.int32, (LANES, LANES), 1)
    return (row + col == LANES - 1).astype(F32).astype(BF16)


def flip_lanes(v, anti):
    pieces = [v[:, i : i + LANES] for i in range(0, v.shape[1], LANES)]
    return jnp.concatenate([dot(p, anti) for p in pieces[::-1]], axis=1)


def inv_rms(v):
    return lax.rsqrt(jnp.mean(v * v, axis=-1, keepdims=True) + 1e-05)


def softplus(v):
    return jnp.maximum(v, 0.0) + jnp.log1p(jnp.exp(-jnp.abs(v)))


def silu(v):
    return v * jax.nn.sigmoid(v)


def kernel(
    x_hbm, gain_hbm, in_hbm, cw_hbm, cb_hbm, sp_hbm, tp_hbm, tb_hbm, decay_hbm, skip_hbm, out_hbm,
    o_ref,
    x_ref, gain_ref, in_ref, gate_ref, cw_ref, cb_ref, sp_ref, tp_ref, tb_ref, decay_ref, skip_ref, out_ref,
    halo, nrm, a2, edge, u_s, proj, proj_t, dt_s, du_s, hist, cblk, cum, gc, pre, sg, gmix,
    send_a, recv_a, send_z, recv_z, send_c, recv_c, hin,
    halo_send, halo_recv, a_send, a_recv, z_send, z_recv, c_send, c_recv, fetched, go,
):
    tokens, width = x_ref.shape
    inner_width = cw_ref.shape[1]
    taps = cw_ref.shape[0]
    rank = tp_ref.shape[0]
    states = decay_ref.shape[0]
    blocks = tokens // ROWS
    slices = inner_width // LANES
    index = lax.axis_index("seq")
    count = GROUP * FAR
    far = index // GROUP
    place = index % GROUP
    left = (index + count - 1) % count
    right = (index + 1) % count
    members = [far * GROUP + (place + d) % GROUP for d in range(1, GROUP)]
    distant = [((far + d) % FAR) * GROUP + place for d in range(1, FAR)]

    barrier = pltpu.get_barrier_semaphore()
    near_z = [distant[0], distant[2]]
    for peer in [left, right] + members + near_z:
        pl.semaphore_signal(
            barrier, inc=1, device_id={"seq": peer}, device_id_type=pl.DeviceIdType.MESH
        )

    def remote(src, dst, send, recv, peer):
        return pltpu.make_async_remote_copy(
            src_ref=src, dst_ref=dst, send_sem=send, recv_sem=recv,
            device_id={"seq": peer}, device_id_type=pl.DeviceIdType.MESH,
        )

    halves = [in_hbm.at[:, pl.ds(i * inner_width, inner_width)] for i in range(2)]
    pairs = [
        (x_hbm, x_ref), (gain_hbm, gain_ref), (halves[0], in_ref), (cw_hbm, cw_ref), (cb_hbm, cb_ref),
        (sp_hbm, sp_ref), (tp_hbm, tp_ref), (tb_hbm, tb_ref), (decay_hbm, decay_ref),
        (halves[1], gate_ref), (skip_hbm, skip_ref), (out_hbm, out_ref),
    ]
    fetches = [pltpu.make_async_copy(src, dst, fetched.at[i]) for i, (src, dst) in enumerate(pairs)]
    for f in fetches:
        f.start()

    def arrive(first, last):
        for f in fetches[first:last]:
            f.wait()

    arrive(0, 2)

    def a2_wide(first=0, last=slices):
        return jnp.concatenate([a2[k] for k in range(first, last)], axis=1)

    anti = anti_identity()
    gain = gain_ref[...]
    x = x_ref[...]
    x32 = x.astype(F32)
    scale = inv_rms(x32)
    nrm[0] = (x32 * scale * gain).astype(BF16)
    nrm[1] = (flip_lanes(x, anti) * scale * gain).astype(BF16)

    def convolve(v, branch, cols):
        total = cb_ref[:, cols]
        size = v.shape[0]
        for k in range(taps):
            back = taps - 1 - k
            shift = back if branch == 0 else (size - back) % size
            moved = v if back == 0 else pltpu.roll(v, shift, 0)
            total = total + cw_ref[k : k + 1, cols] * moved
        return silu(total).astype(BF16)

    wide = 256
    arrive(2, 9)
    for k in range(slices):
        a2[k] = decay_ref[:, k * LANES : (k + 1) * LANES] * (-LOG2E)

    def front(i, _):
        cols = pl.ds(pl.multiple_of(i * wide, wide), wide)
        for branch in range(2):
            inner = dot(nrm[branch], in_ref[:, cols])
            edge[branch, :, cols] = inner[:ROWS] if branch == 0 else inner[tokens - ROWS :]
            u_s[branch, :, cols] = convolve(inner, branch, cols).astype(F32)
        return 0

    lax.fori_loop(0, inner_width // wide, front, 0)

    for branch in range(2):
        proj[branch] = dot_nt(u_s[branch].astype(BF16), sp_ref[...])

    def steps(i, _):
        cols = pl.ds(pl.multiple_of(i * wide, wide), wide)
        for branch in range(2):
            low = proj[branch, :, :rank].astype(BF16)
            dt = softplus(dot(low, tp_ref[:, cols]) + tb_ref[:, cols])
            dt_s[branch, :, cols] = dt
            du_s[branch, :, cols] = dt * u_s[branch, :, cols]
        return 0

    lax.fori_loop(0, inner_width // wide, steps, 0)

    pl.semaphore_wait(barrier, 2 + len(members) + len(near_z))
    edge_rows = halo.shape[1]
    to_right = remote(
        x_hbm.at[pl.ds(tokens - edge_rows, edge_rows)], halo.at[0], halo_send.at[0], halo_recv.at[0], right
    )
    to_left = remote(x_hbm.at[pl.ds(0, edge_rows)], halo.at[1], halo_send.at[1], halo_recv.at[1], left)
    to_right.start()
    to_left.start()
    for peer in near_z:
        pl.semaphore_signal(go, inc=1, device_id={"seq": peer}, device_id_type=pl.DeviceIdType.MESH)

    def turn_proj():
        proj_t[...] = jnp.concatenate([proj[0], proj[1]], axis=1).T

    proj_width = proj.shape[2]
    turn_proj()
    half = slices // 2

    def scan(first, last):
        ends = []
        for part in range(2):
            lanes = pl.ds(part * half * LANES, half * LANES)
            rate = a2_wide(part * half, (part + 1) * half)

            def chunk(c, carried, lanes=lanes, rate=rate):
                carried = list(carried)
                base = c * ROWS
                rolled = [
                    pltpu.roll(proj_t[rank : rank + states, :], (tokens - base) % tokens, 1),
                    pltpu.roll(
                        proj_t[proj_width + rank : proj_width + rank + states, :],
                        (base + ROWS) % tokens, 1,
                    ),
                ]
                for j in range(ROWS):
                    for branch in range(2):
                        t = base + j if branch == 0 else tokens - 1 - base - j
                        pick = j if branch == 0 else ROWS - 1 - j
                        column = jnp.broadcast_to(rolled[branch][:, pick : pick + 1], (states, LANES))
                        column = jnp.concatenate([column] * half, axis=1)
                        dt = jnp.broadcast_to(dt_s[branch, pl.ds(t, 1), lanes], (states, half * LANES))
                        du = jnp.broadcast_to(du_s[branch, pl.ds(t, 1), lanes], (states, half * LANES))
                        h = jnp.exp2(dt * rate) * carried[branch] + du * column
                        hist[branch, pl.ds(pl.multiple_of(t * states, states), states), lanes] = h.astype(BF16)
                        carried[branch] = h
                return tuple(carried)

            zero = jnp.zeros((states, half * LANES), F32)
            ends.append(lax.fori_loop(first, last, chunk, (zero, zero)))
        return ends

    main = scan(1, blocks)
    for part in range(2):
        for branch in range(2):
            for k in range(half):
                hin[branch, part * half + k] = main[part][branch][:, k * LANES : (k + 1) * LANES]

    to_right.wait()
    to_left.wait()
    border = halo[...]
    near = border[0].astype(F32)
    far_side = border[1]
    far32 = far_side.astype(F32)
    ahead = (near * inv_rms(near) * gain).astype(BF16)
    behind = (flip_lanes(far_side, anti) * inv_rms(far32) * gain).astype(BF16)
    has_left = (index > 0).astype(F32)
    has_right = (index < count - 1).astype(F32)

    def border_front(i, _):
        cols = pl.ds(pl.multiple_of(i * wide, wide), wide)
        weights = in_ref[:, cols]
        v = dot(ahead, weights)[edge_rows - ROWS :] * has_left
        joined = jnp.concatenate([v, edge[0, :, cols]], axis=0)
        u_s[0, 0:ROWS, cols] = convolve(joined, 0, cols).astype(F32)[ROWS:]
        v = dot(behind, weights)[:ROWS] * has_right
        joined = jnp.concatenate([edge[1, :, cols], v], axis=0)
        u_s[1, tokens - ROWS : tokens, cols] = convolve(joined, 1, cols).astype(F32)[:ROWS]
        return 0

    lax.fori_loop(0, inner_width // wide, border_front, 0)
    border_u = jnp.concatenate([u_s[0, 0:ROWS], u_s[1, tokens - ROWS : tokens]], axis=0)
    border_p = dot_nt(border_u.astype(BF16), sp_ref[...])
    proj[0, 0:ROWS] = border_p[:ROWS]
    proj[1, tokens - ROWS : tokens] = border_p[ROWS:]
    border_dt = softplus(dot(border_p[:, :rank].astype(BF16), tp_ref[...]) + tb_ref[...])
    border_du = border_dt * border_u
    dt_s[0, 0:ROWS] = border_dt[:ROWS]
    dt_s[1, tokens - ROWS : tokens] = border_dt[ROWS:]
    du_s[0, 0:ROWS] = border_du[:ROWS]
    du_s[1, tokens - ROWS : tokens] = border_du[ROWS:]
    turn_proj()
    start = scan(0, 1)

    def wide_tile(rows):
        return jnp.concatenate(rows + [jnp.zeros((16 - len(rows), LANES), F32)], axis=0)

    main_tot = [
        jnp.sum(dt_s[0, ROWS:tokens], axis=0, keepdims=True),
        jnp.sum(dt_s[1, 0 : tokens - ROWS], axis=0, keepdims=True),
    ]
    start_tot = [
        jnp.sum(border_dt[:ROWS], axis=0, keepdims=True),
        jnp.sum(border_dt[ROWS:], axis=0, keepdims=True),
    ]

    def tot_rows(values):
        rows = []
        for v in values:
            high = v.astype(BF16).astype(F32)
            rows += [high, v - high]
        return wide_tile(rows).astype(BF16)

    for k in range(slices):
        lanes = slice(k * LANES, (k + 1) * LANES)
        part, inside = divmod(k, half)
        own = slice(inside * LANES, (inside + 1) * LANES)
        for branch in range(2):
            first = start[part][branch][:, own]
            grown = jnp.exp2(main_tot[branch][:, lanes] * a2[k]) * first + hin[branch, k]
            send_a[k, branch] = grown.astype(BF16)
            hist_keep = first
            hin[branch, k] = hist_keep
        send_a[k, 2] = tot_rows([(main_tot[b] + start_tot[b])[:, lanes] for b in range(2)])

    copies_a = []
    for d, peer in enumerate(members):
        target = (place + d + 1) % GROUP
        copies_a.append(
            remote(send_a.at[target], recv_a.at[place], a_send.at[d], a_recv.at[d], peer)
        )
    for c in copies_a:
        c.start()
    recv_a[place] = send_a[place]
    recv_z[far] = jnp.zeros(recv_z.shape[1:], BF16)

    arrive(9, len(fetches))

    def gates(i, _):
        cols = pl.ds(pl.multiple_of(i * wide, wide), wide)
        for branch in range(2):
            sg[branch, :, cols] = silu(dot(nrm[branch], gate_ref[:, cols]))
        return 0

    lax.fori_loop(0, inner_width // wide, gates, 0)

    for c in copies_a:
        c.wait()

    rate = a2[place]
    got_s = [[recv_a[m, b].astype(F32) for m in range(GROUP)] for b in range(2)]
    got_t = []
    for m in range(GROUP):
        rows = recv_a[m, 2].astype(F32)
        got_t.append([rows[0:1] + rows[1:2], rows[2:3] + rows[3:4]])

    prefix = [[None] * GROUP, [None] * GROUP]
    before = [[None] * GROUP, [None] * GROUP]
    for branch in range(2):
        state = jnp.zeros((states, LANES), F32)
        total = jnp.zeros((1, LANES), F32)
        order = range(GROUP) if branch == 0 else range(GROUP - 1, -1, -1)
        for m in order:
            prefix[branch][m] = state
            before[branch][m] = total
            state = jnp.exp2(got_t[m][branch] * rate) * state + got_s[branch][m]
            total = total + got_t[m][branch]
        send_z[branch, 0] = state.astype(BF16)
        send_z[branch, 1] = tot_rows([total])

    pl.semaphore_wait(go, len(near_z))
    copies_z = []
    for d, peer in enumerate(distant):
        target = (far + d + 1) % FAR
        branch = (target < far).astype(jnp.int32)
        copies_z.append(
            remote(send_z.at[branch], recv_z.at[far], z_send.at[d], z_recv.at[d], peer)
        )
    for c in copies_z:
        c.start()

    t_row = lax.broadcasted_iota(jnp.int32, (tokens, tokens), 0)
    t_col = lax.broadcasted_iota(jnp.int32, (tokens, tokens), 1)
    below = [
        (t_col <= t_row) & ((t_col < ROWS) == (t_row < ROWS)),
        (t_col >= t_row) & ((t_col >= tokens - ROWS) == (t_row >= tokens - ROWS)),
    ]
    for branch in range(2):
        ones = below[branch].astype(F32).astype(BF16)
        high, low = split2(dt_s[branch])
        cum[branch] = dot(ones, high) + dot(ones, low)

    c_first = rank + states
    pick_row = lax.broadcasted_iota(jnp.int32, (states, 256), 0)
    pick_col = lax.broadcasted_iota(jnp.int32, (states, 256), 1)
    spread = (pick_col % states == pick_row).astype(F32).astype(BF16)
    own_row = lax.broadcasted_iota(jnp.int32, (tokens, 256), 0)
    own_col = lax.broadcasted_iota(jnp.int32, (tokens, 256), 1)
    own = own_col // states == own_row % (256 // states)
    for branch in range(2):
        maps = proj[branch, :, c_first : c_first + states].astype(BF16)
        cblk[branch] = jnp.where(own, dot(maps, spread), 0.0).astype(BF16)

    run = 256 // states

    def local_out(i, _):
        rows = pl.ds(pl.multiple_of(i * run, run), run)
        deep = pl.ds(pl.multiple_of(i * 256, 256), 256)
        for branch in range(2):
            local = dot(cblk[branch, rows, :], hist[branch, deep, :])
            pre[branch, rows, :] = local + skip_ref[...] * u_s[branch, rows, :]
        return 0

    lax.fori_loop(0, tokens // run, local_out, 0)

    def factors(i, _):
        rows = pl.ds(pl.multiple_of(i * ROWS, ROWS), ROWS)
        for branch in range(2):
            maps = proj[branch, rows, :]
            for n in range(states):
                c_col = jnp.broadcast_to(maps[:, c_first + n : c_first + n + 1], (ROWS, LANES))
                for k in range(slices):
                    seen = cum[branch, rows, k * LANES : (k + 1) * LANES]
                    gc[branch, k, n, rows, :] = jnp.exp2(seen * a2[k, n : n + 1, :]) * c_col
        return 0

    lax.fori_loop(0, blocks, factors, 0)

    for c in copies_z:
        c.wait()

    for branch in range(2):
        state = jnp.zeros((states, LANES), F32)
        order = range(FAR) if branch == 0 else range(FAR - 1, -1, -1)
        for z in order:
            here = (z < far) if branch == 0 else (z > far)
            rows = recv_z[z, 1].astype(F32)
            later = jnp.exp2((rows[0:1] + rows[1:2]) * rate) * state + recv_z[z, 0].astype(F32)
            state = jnp.where(here, later, state)
        for m in range(GROUP):
            entering = jnp.exp2(before[branch][m] * rate) * state + prefix[branch][m]
            send_c[m, branch] = entering.astype(BF16)

    copies_c = []
    for d, peer in enumerate(members):
        target = (place + d + 1) % GROUP
        copies_c.append(
            remote(send_c.at[target], recv_c.at[place], c_send.at[d], c_recv.at[d], peer)
        )
    for c in copies_c:
        c.start()
    recv_c[place] = send_c[place]
    for c in copies_c:
        c.wait()

    for branch in range(2):
        for k in range(slices):
            entering = recv_c[k, branch].astype(F32)
            gone = jnp.exp2(start_tot[branch][:, k * LANES : (k + 1) * LANES] * a2[k])
            hin[branch, k] = gone * entering + hin[branch, k]

    def finish(k, _):
        cols = pl.ds(pl.multiple_of(k * LANES, LANES), LANES)
        for branch in range(2):
            spread_h = [
                jnp.broadcast_to(hin[branch, k, n : n + 1, :], (ROWS, LANES)) for n in range(states)
            ]
            edge_h = recv_c[k, branch].astype(F32)
            border_block = 0 if branch == 0 else blocks - 1
            pieces = []
            for b in range(blocks):
                rows = slice(b * ROWS, (b + 1) * ROWS)
                total = pre[branch, rows, cols]
                for n in range(states):
                    if b == border_block:
                        h = jnp.broadcast_to(edge_h[n : n + 1, :], (ROWS, LANES))
                    else:
                        h = spread_h[n]
                    total = total + gc[branch, k, n, rows, :] * h
                pieces.append(total * sg[branch, rows, cols])
                if len(pieces) == 2:
                    gmix[branch, (b - 1) * ROWS : (b + 1) * ROWS, cols] = jnp.concatenate(
                        pieces, axis=0
                    ).astype(BF16)
                    pieces = []
        return 0

    lax.fori_loop(0, slices, finish, 0)
    forward = dot(gmix[0], out_ref[...]).astype(BF16)
    flipped = flip_lanes(dot(gmix[1], out_ref[...]).astype(BF16), anti)
    o_ref[...] = forward.astype(F32) + flipped


def shards(
    residual_stream, norm_gain, in_proj, conv_weight, conv_bias, state_proj, step_proj,
    step_bias, decay_rate, skip_gain, out_proj,
):
    tokens, width = residual_stream.shape
    inner_width = conv_weight.shape[1]
    states = decay_rate.shape[1]
    rank = step_proj.shape[0]
    columns = state_proj.shape[1]
    slices = inner_width // LANES
    hbm = pl.BlockSpec(memory_space=pl.ANY)
    vmem = pl.BlockSpec(memory_space=pltpu.VMEM)
    by_token = (2, tokens, inner_width)
    scratch = [
        pltpu.VMEM((tokens, width), BF16),
        pltpu.VMEM((1, width), F32),
        pltpu.VMEM((width, inner_width), BF16),
        pltpu.VMEM((width, inner_width), BF16),
        pltpu.VMEM(conv_weight.shape, F32),
        pltpu.VMEM((1, inner_width), F32),
        pltpu.VMEM((columns, inner_width), BF16),
        pltpu.VMEM((rank, inner_width), BF16),
        pltpu.VMEM((1, inner_width), F32),
        pltpu.VMEM((states, inner_width), F32),
        pltpu.VMEM((1, inner_width), F32),
        pltpu.VMEM((inner_width, width), BF16),
        pltpu.VMEM((2, 16, width), BF16),
        pltpu.VMEM((2, tokens, width), BF16),
        pltpu.VMEM((slices, states, LANES), F32),
        pltpu.VMEM((2, ROWS, inner_width), F32),
        pltpu.VMEM(by_token, F32),
        pltpu.VMEM((2, tokens, state_proj.shape[1]), F32),
        pltpu.VMEM((2 * state_proj.shape[1], tokens), F32),
        pltpu.VMEM(by_token, F32),
        pltpu.VMEM(by_token, F32),
        pltpu.VMEM((2, tokens * states, inner_width), BF16),
        pltpu.VMEM((2, tokens, 256), BF16),
        pltpu.VMEM(by_token, F32),
        pltpu.VMEM((2, slices, states, tokens, LANES), F32),
        pltpu.VMEM(by_token, F32),
        pltpu.VMEM(by_token, F32),
        pltpu.VMEM(by_token, BF16),
        pltpu.VMEM((GROUP, 3, states, LANES), BF16),
        pltpu.VMEM((GROUP, 3, states, LANES), BF16),
        pltpu.VMEM((2, 2, states, LANES), BF16),
        pltpu.VMEM((FAR, 2, states, LANES), BF16),
        pltpu.VMEM((GROUP, 2, states, LANES), BF16),
        pltpu.VMEM((GROUP, 2, states, LANES), BF16),
        pltpu.VMEM((2, slices, states, LANES), F32),
        pltpu.SemaphoreType.DMA((2,)),
        pltpu.SemaphoreType.DMA((2,)),
        pltpu.SemaphoreType.DMA((GROUP - 1,)),
        pltpu.SemaphoreType.DMA((GROUP - 1,)),
        pltpu.SemaphoreType.DMA((FAR - 1,)),
        pltpu.SemaphoreType.DMA((FAR - 1,)),
        pltpu.SemaphoreType.DMA((GROUP - 1,)),
        pltpu.SemaphoreType.DMA((GROUP - 1,)),
        pltpu.SemaphoreType.DMA((12,)),
        pltpu.SemaphoreType.REGULAR,
    ]
    mixed = pl.pallas_call(
        kernel,
        out_shape=jax.ShapeDtypeStruct((tokens, width), F32),
        in_specs=[hbm] * 11,
        out_specs=vmem,
        scratch_shapes=scratch,
        compiler_params=pltpu.CompilerParams(
            collective_id=0, has_side_effects=True, vmem_limit_bytes=60 << 20
        ),
    )(
        residual_stream,
        norm_gain.reshape(1, -1),
        in_proj,
        conv_weight,
        conv_bias.reshape(1, -1),
        state_proj.T,
        step_proj,
        step_bias.reshape(1, -1),
        decay_rate.T,
        skip_gain.reshape(1, -1),
        out_proj,
    )
    return (residual_stream.astype(F32) + mixed).astype(BF16)


def solution(mesh):
    return jax.shard_map(
        shards,
        mesh=mesh,
        in_specs=(P(("dp", "seq"), None), P(), P(), P(), P(), P(), P(), P(), P(), P(), P()),
        out_specs=P(("dp", "seq"), None),
        check_vma=False,
    )
```

```python
import functools
import math

import jax
import jax.numpy as jnp
from jax import lax
from jax.experimental import pallas as pl
from jax.experimental.pallas import tpu as pltpu
from jax.sharding import PartitionSpec as P

F32 = jnp.float32
BF16 = jnp.bfloat16
LOG2E = math.log2(math.e)
GROUP = 8
FAR = 4
LANES = 128
ROWS = 8
SCAN = 40
EARLY = 7


def dot(a, b):
    return jnp.dot(a, b, preferred_element_type=F32)


def dot_nt(a, b):
    return lax.dot_general(a, b, (((1,), (1,)), ((), ())), preferred_element_type=F32)


def split2(v):
    high = v.astype(BF16)
    return high, (v - high.astype(F32)).astype(BF16)


def anti_identity():
    row = lax.broadcasted_iota(jnp.int32, (LANES, LANES), 0)
    col = lax.broadcasted_iota(jnp.int32, (LANES, LANES), 1)
    return (row + col == LANES - 1).astype(F32).astype(BF16)


def flip_lanes(v, anti):
    pieces = [v[:, i : i + LANES] for i in range(0, v.shape[1], LANES)]
    return jnp.concatenate([dot(p, anti) for p in pieces[::-1]], axis=1)


def inv_rms(v):
    return lax.rsqrt(jnp.mean(v * v, axis=-1, keepdims=True) + 1e-05)


def softplus(v):
    return jnp.maximum(v, 0.0) + jnp.log1p(jnp.exp(-jnp.abs(v)))


def silu(v):
    return v * jax.nn.sigmoid(v)


def kernel(
    x_hbm, gain_hbm, in_hbm, cw_hbm, cb_hbm, sp_hbm, tp_hbm, tb_hbm, decay_hbm, skip_hbm, out_hbm,
    o_ref,
    x_ref, gain_ref, in_ref, gate_ref, cw_ref, cb_ref, sp_ref, tp_ref, tb_ref, decay_ref, skip_ref, out_ref,
    halo, nrm, a2, edge, u_s, proj, proj_t, dt_s, du_s, hist, cblk, cum, gc, pre, sg, gmix,
    send_a, recv_a, send_z, recv_z, send_c, recv_c, hin, first_tot,
    halo_send, halo_recv, a_send, a_recv, z_send, z_recv, c_send, c_recv, fetched, go,
):
    tokens, width = x_ref.shape
    inner_width = cw_ref.shape[1]
    taps = cw_ref.shape[0]
    rank = tp_ref.shape[0]
    states = decay_ref.shape[0]
    blocks = tokens // ROWS
    slices = inner_width // LANES
    index = lax.axis_index("seq")
    count = GROUP * FAR
    far = index // GROUP
    place = index % GROUP
    left = (index + count - 1) % count
    right = (index + 1) % count
    members = [far * GROUP + (place + d) % GROUP for d in range(1, GROUP)]
    distant = [((far + d) % FAR) * GROUP + place for d in range(1, FAR)]

    barrier = pltpu.get_barrier_semaphore()
    near_z = [distant[0], distant[2]]
    for peer in [left, right] + members + near_z:
        pl.semaphore_signal(
            barrier, inc=1, device_id={"seq": peer}, device_id_type=pl.DeviceIdType.MESH
        )

    def remote(src, dst, send, recv, peer):
        return pltpu.make_async_remote_copy(
            src_ref=src, dst_ref=dst, send_sem=send, recv_sem=recv,
            device_id={"seq": peer}, device_id_type=pl.DeviceIdType.MESH,
        )

    halves = [in_hbm.at[:, pl.ds(i * inner_width, inner_width)] for i in range(2)]
    pairs = [
        (x_hbm, x_ref), (gain_hbm, gain_ref), (halves[0], in_ref), (cw_hbm, cw_ref), (cb_hbm, cb_ref),
        (sp_hbm, sp_ref), (tp_hbm, tp_ref), (tb_hbm, tb_ref), (decay_hbm, decay_ref),
        (halves[1], gate_ref), (skip_hbm, skip_ref), (out_hbm, out_ref),
    ]
    fetches = [pltpu.make_async_copy(src, dst, fetched.at[i]) for i, (src, dst) in enumerate(pairs)]
    for f in fetches:
        f.start()

    def arrive(first, last):
        for f in fetches[first:last]:
            f.wait()

    arrive(0, 2)

    def a2_wide(first=0, last=slices):
        return jnp.concatenate([a2[k] for k in range(first, last)], axis=1)

    anti = anti_identity()
    gain = gain_ref[...]
    x = x_ref[...]
    x32 = x.astype(F32)
    scale = inv_rms(x32)
    nrm[0] = (x32 * scale * gain).astype(BF16)
    nrm[1] = (flip_lanes(x, anti) * scale * gain).astype(BF16)

    def convolve(v, branch, cols):
        total = cb_ref[:, cols]
        size = v.shape[0]
        for k in range(taps):
            back = taps - 1 - k
            shift = back if branch == 0 else (size - back) % size
            moved = v if back == 0 else pltpu.roll(v, shift, 0)
            total = total + cw_ref[k : k + 1, cols] * moved
        return silu(total).astype(BF16)

    wide = 256
    arrive(2, 9)
    for k in range(slices):
        a2[k] = decay_ref[:, k * LANES : (k + 1) * LANES] * (-LOG2E)

    def front(i, _):
        cols = pl.ds(pl.multiple_of(i * wide, wide), wide)
        for branch in range(2):
            inner = dot(nrm[branch], in_ref[:, cols])
            edge[branch, :, cols] = inner[:ROWS] if branch == 0 else inner[tokens - ROWS :]
            u_s[branch, :, cols] = convolve(inner, branch, cols).astype(F32)
        return 0

    lax.fori_loop(0, inner_width // wide, front, 0)

    for branch in range(2):
        proj[branch] = dot_nt(u_s[branch].astype(BF16), sp_ref[...])

    def steps(i, _):
        cols = pl.ds(pl.multiple_of(i * wide, wide), wide)
        for branch in range(2):
            low = proj[branch, :, :rank].astype(BF16)
            dt = softplus(dot(low, tp_ref[:, cols]) + tb_ref[:, cols])
            dt_s[branch, :, cols] = dt
            du_s[branch, :, cols] = (dt * u_s[branch, :, cols]).astype(BF16)
        return 0

    lax.fori_loop(0, inner_width // wide, steps, 0)

    pl.semaphore_wait(barrier, 2 + len(members) + len(near_z))
    edge_rows = halo.shape[1]
    to_right = remote(
        x_hbm.at[pl.ds(tokens - edge_rows, edge_rows)], halo.at[0], halo_send.at[0], halo_recv.at[0], right
    )
    to_left = remote(x_hbm.at[pl.ds(0, edge_rows)], halo.at[1], halo_send.at[1], halo_recv.at[1], left)
    to_right.start()
    to_left.start()
    for peer in near_z:
        pl.semaphore_signal(go, inc=1, device_id={"seq": peer}, device_id_type=pl.DeviceIdType.MESH)

    def turn_proj():
        proj_t[...] = jnp.concatenate([proj[0], proj[1]], axis=1).T

    proj_width = proj.shape[2]
    turn_proj()
    half = slices // 2

    lane = lax.broadcasted_iota(jnp.int32, (states, tokens), 1)

    def scan(first, last, size):
        ends = []
        for part in range(2):
            lanes = pl.ds(part * half * LANES, half * LANES)
            rate = a2_wide(part * half, (part + 1) * half)

            def chunk(c, carried, lanes=lanes, rate=rate):
                carried = list(carried)
                base = first * ROWS + c * size
                times = [[base + j, tokens - 1 - base - j] for j in range(size)]
                added = []
                for branch in range(2):
                    top = branch * proj_width + rank
                    maps = proj_t[top : top + states, :]
                    tiles = [jnp.where(lane == t[branch], maps, 0.0).astype(BF16) for t in times]
                    added.append(dot(jnp.concatenate(tiles, axis=0), du_s[branch, :, lanes]))
                for j in range(size):
                    for branch in range(2):
                        t = times[j][branch]
                        dt = jnp.broadcast_to(dt_s[branch, pl.ds(t, 1), lanes], (states, half * LANES))
                        new = added[branch][j * states : (j + 1) * states]
                        h = jnp.exp2(dt * rate) * carried[branch] + new
                        hist[branch, pl.ds(pl.multiple_of(t * states, states), states), lanes] = h.astype(BF16)
                        carried[branch] = h
                return tuple(carried)

            zero = jnp.zeros((states, half * LANES), F32)
            trips = (last - first) * ROWS // size
            ends.append(lax.fori_loop(0, trips, chunk, (zero, zero)))
        return ends

    main = scan(1, blocks, SCAN)
    for part in range(2):
        for branch in range(2):
            for k in range(half):
                hin[branch, part * half + k] = main[part][branch][:, k * LANES : (k + 1) * LANES]

    to_right.wait()
    to_left.wait()
    border = halo[...]
    near = border[0].astype(F32)
    far_side = border[1]
    far32 = far_side.astype(F32)
    ahead = (near * inv_rms(near) * gain).astype(BF16)
    behind = (flip_lanes(far_side, anti) * inv_rms(far32) * gain).astype(BF16)
    has_left = (index > 0).astype(F32)
    has_right = (index < count - 1).astype(F32)

    def border_front(i, _):
        cols = pl.ds(pl.multiple_of(i * wide, wide), wide)
        weights = in_ref[:, cols]
        v = dot(ahead, weights)[edge_rows - ROWS :] * has_left
        joined = jnp.concatenate([v, edge[0, :, cols]], axis=0)
        u_s[0, 0:ROWS, cols] = convolve(joined, 0, cols).astype(F32)[ROWS:]
        v = dot(behind, weights)[:ROWS] * has_right
        joined = jnp.concatenate([edge[1, :, cols], v], axis=0)
        u_s[1, tokens - ROWS : tokens, cols] = convolve(joined, 1, cols).astype(F32)[:ROWS]
        return 0

    lax.fori_loop(0, inner_width // wide, border_front, 0)
    border_u = jnp.concatenate([u_s[0, 0:ROWS], u_s[1, tokens - ROWS : tokens]], axis=0)
    border_p = dot_nt(border_u.astype(BF16), sp_ref[...])
    proj[0, 0:ROWS] = border_p[:ROWS]
    proj[1, tokens - ROWS : tokens] = border_p[ROWS:]
    border_dt = softplus(dot(border_p[:, :rank].astype(BF16), tp_ref[...]) + tb_ref[...])
    border_du = border_dt * border_u
    dt_s[0, 0:ROWS] = border_dt[:ROWS]
    dt_s[1, tokens - ROWS : tokens] = border_dt[ROWS:]
    none = jnp.zeros((tokens - ROWS, inner_width), F32)
    du_s[0] = jnp.concatenate([border_du[:ROWS], none], axis=0).astype(BF16)
    du_s[1] = jnp.concatenate([none, border_du[ROWS:]], axis=0).astype(BF16)
    turn_proj()
    start = scan(0, 1, ROWS)

    def wide_tile(rows):
        return jnp.concatenate(rows + [jnp.zeros((16 - len(rows), LANES), F32)], axis=0)

    main_tot = [
        jnp.sum(dt_s[0, ROWS:tokens], axis=0, keepdims=True),
        jnp.sum(dt_s[1, 0 : tokens - ROWS], axis=0, keepdims=True),
    ]
    start_tot = [
        jnp.sum(border_dt[:ROWS], axis=0, keepdims=True),
        jnp.sum(border_dt[ROWS:], axis=0, keepdims=True),
    ]

    def tot_rows(values):
        rows = []
        for v in values:
            high = v.astype(BF16).astype(F32)
            rows += [high, v - high]
        return wide_tile(rows).astype(BF16)

    for k in range(slices):
        lanes = slice(k * LANES, (k + 1) * LANES)
        part, inside = divmod(k, half)
        own = slice(inside * LANES, (inside + 1) * LANES)
        for branch in range(2):
            first = start[part][branch][:, own]
            grown = jnp.exp2(main_tot[branch][:, lanes] * a2[k]) * first + hin[branch, k]
            send_a[k, branch] = grown.astype(BF16)
            hist_keep = first
            hin[branch, k] = hist_keep
        send_a[k, 2] = tot_rows([(main_tot[b] + start_tot[b])[:, lanes] for b in range(2)])
        for branch in range(2):
            first_tot[k, branch] = jnp.broadcast_to(start_tot[branch][:, lanes], (ROWS, LANES))

    copies_a = []
    for d, peer in enumerate(members):
        target = (place + d + 1) % GROUP
        copies_a.append(
            remote(send_a.at[target], recv_a.at[place], a_send.at[d], a_recv.at[d], peer)
        )
    for c in copies_a:
        c.start()
    recv_a[place] = send_a[place]
    recv_z[far] = jnp.zeros(recv_z.shape[1:], BF16)

    arrive(9, len(fetches))

    def gates(i, _):
        cols = pl.ds(pl.multiple_of(i * wide, wide), wide)
        for branch in range(2):
            sg[branch, :, cols] = silu(dot(nrm[branch], gate_ref[:, cols]))
        return 0

    lax.fori_loop(0, inner_width // wide, gates, 0)

    t_row = lax.broadcasted_iota(jnp.int32, (tokens, tokens), 0)
    t_col = lax.broadcasted_iota(jnp.int32, (tokens, tokens), 1)
    below = [
        (t_col <= t_row) & ((t_col < ROWS) == (t_row < ROWS)),
        (t_col >= t_row) & ((t_col >= tokens - ROWS) == (t_row >= tokens - ROWS)),
    ]
    for branch in range(2):
        ones = below[branch].astype(F32).astype(BF16)
        high, low = split2(dt_s[branch])
        cum[branch] = dot(ones, high) + dot(ones, low)

    c_first = rank + states
    pick_row = lax.broadcasted_iota(jnp.int32, (states, 256), 0)
    pick_col = lax.broadcasted_iota(jnp.int32, (states, 256), 1)
    spread = (pick_col % states == pick_row).astype(F32).astype(BF16)
    own_row = lax.broadcasted_iota(jnp.int32, (tokens, 256), 0)
    own_col = lax.broadcasted_iota(jnp.int32, (tokens, 256), 1)
    own = own_col // states == own_row % (256 // states)
    for branch in range(2):
        maps = proj[branch, :, c_first : c_first + states].astype(BF16)
        cblk[branch] = jnp.where(own, dot(maps, spread), 0.0).astype(BF16)

    run = 256 // states

    def local_out(i, _):
        rows = pl.ds(pl.multiple_of(i * run, run), run)
        deep = pl.ds(pl.multiple_of(i * 256, 256), 256)
        for branch in range(2):
            local = dot(cblk[branch, rows, :], hist[branch, deep, :])
            pre[branch, rows, :] = local + skip_ref[...] * u_s[branch, rows, :]
        return 0

    lax.fori_loop(0, tokens // run, local_out, 0)

    def factors(i, _):
        rows = pl.ds(pl.multiple_of(i * ROWS, ROWS), ROWS)
        for branch in range(2):
            maps = proj[branch, rows, :]
            for n in range(states):
                c_col = jnp.broadcast_to(maps[:, c_first + n : c_first + n + 1], (ROWS, LANES))
                for k in range(slices):
                    seen = cum[branch, rows, k * LANES : (k + 1) * LANES]
                    gc[branch, k, n, rows, :] = jnp.exp2(seen * a2[k, n : n + 1, :]) * c_col
        return 0

    lax.fori_loop(0, EARLY, factors, 0)

    for c in copies_a:
        c.wait()

    rate = a2[place]
    got_s = [[recv_a[m, b].astype(F32) for m in range(GROUP)] for b in range(2)]
    got_t = []
    for m in range(GROUP):
        rows = recv_a[m, 2].astype(F32)
        got_t.append([rows[0:1] + rows[1:2], rows[2:3] + rows[3:4]])

    prefix = [[None] * GROUP, [None] * GROUP]
    before = [[None] * GROUP, [None] * GROUP]
    for branch in range(2):
        state = jnp.zeros((states, LANES), F32)
        total = jnp.zeros((1, LANES), F32)
        order = range(GROUP) if branch == 0 else range(GROUP - 1, -1, -1)
        for m in order:
            prefix[branch][m] = state
            before[branch][m] = total
            state = jnp.exp2(got_t[m][branch] * rate) * state + got_s[branch][m]
            total = total + got_t[m][branch]
        send_z[branch, 0] = state.astype(BF16)
        send_z[branch, 1] = tot_rows([total])

    pl.semaphore_wait(go, len(near_z))
    copies_z = []
    for d, peer in enumerate(distant):
        target = (far + d + 1) % FAR
        branch = (target < far).astype(jnp.int32)
        copies_z.append(
            remote(send_z.at[branch], recv_z.at[far], z_send.at[d], z_recv.at[d], peer)
        )
    for c in copies_z:
        c.start()

    lax.fori_loop(EARLY, blocks, factors, 0)

    for c in copies_z:
        c.wait()

    for branch in range(2):
        state = jnp.zeros((states, LANES), F32)
        order = range(FAR) if branch == 0 else range(FAR - 1, -1, -1)
        for z in order:
            here = (z < far) if branch == 0 else (z > far)
            rows = recv_z[z, 1].astype(F32)
            later = jnp.exp2((rows[0:1] + rows[1:2]) * rate) * state + recv_z[z, 0].astype(F32)
            state = jnp.where(here, later, state)
        for m in range(GROUP):
            entering = jnp.exp2(before[branch][m] * rate) * state + prefix[branch][m]
            send_c[m, branch] = entering.astype(BF16)

    def back(d):
        target = (place + d) % GROUP
        return remote(
            send_c.at[target], recv_c.at[place], c_send.at[d - 1], c_recv.at[d - 1], far * GROUP + target
        )

    for d in range(1, GROUP):
        back(d).start()
    recv_c[place] = send_c[place]

    def finish(k):
        cols = pl.ds(pl.multiple_of(k * LANES, LANES), LANES)
        for branch in range(2):
            edge_h = recv_c[k, branch].astype(F32)
            gone = jnp.exp2(first_tot[k, branch, 0:1, :] * a2[k])
            main_h = gone * edge_h + hin[branch, k]
            spread_h = [jnp.broadcast_to(main_h[n : n + 1, :], (ROWS, LANES)) for n in range(states)]
            border_block = 0 if branch == 0 else blocks - 1
            pieces = []
            for b in range(blocks):
                rows = slice(b * ROWS, (b + 1) * ROWS)
                total = pre[branch, rows, cols]
                for n in range(states):
                    if b == border_block:
                        h = jnp.broadcast_to(edge_h[n : n + 1, :], (ROWS, LANES))
                    else:
                        h = spread_h[n]
                    total = total + gc[branch, k, n, rows, :] * h
                pieces.append(total * sg[branch, rows, cols])
                if len(pieces) == 2:
                    gmix[branch, (b - 1) * ROWS : (b + 1) * ROWS, cols] = jnp.concatenate(
                        pieces, axis=0
                    ).astype(BF16)
                    pieces = []

    def finish_next(d, _):
        back(d).wait()
        finish((place + GROUP - d) % GROUP)
        return 0

    finish(place)
    lax.fori_loop(1, GROUP, finish_next, 0)
    forward = dot(gmix[0], out_ref[...]).astype(BF16)
    flipped = flip_lanes(dot(gmix[1], out_ref[...]).astype(BF16), anti)
    o_ref[...] = forward.astype(F32) + flipped


def shards(
    residual_stream, norm_gain, in_proj, conv_weight, conv_bias, state_proj, step_proj,
    step_bias, decay_rate, skip_gain, out_proj,
):
    tokens, width = residual_stream.shape
    inner_width = conv_weight.shape[1]
    states = decay_rate.shape[1]
    rank = step_proj.shape[0]
    columns = state_proj.shape[1]
    slices = inner_width // LANES
    hbm = pl.BlockSpec(memory_space=pl.ANY)
    vmem = pl.BlockSpec(memory_space=pltpu.VMEM)
    by_token = (2, tokens, inner_width)
    scratch = [
        pltpu.VMEM((tokens, width), BF16),
        pltpu.VMEM((1, width), F32),
        pltpu.VMEM((width, inner_width), BF16),
        pltpu.VMEM((width, inner_width), BF16),
        pltpu.VMEM(conv_weight.shape, F32),
        pltpu.VMEM((1, inner_width), F32),
        pltpu.VMEM((columns, inner_width), BF16),
        pltpu.VMEM((rank, inner_width), BF16),
        pltpu.VMEM((1, inner_width), F32),
        pltpu.VMEM((states, inner_width), F32),
        pltpu.VMEM((1, inner_width), F32),
        pltpu.VMEM((inner_width, width), BF16),
        pltpu.VMEM((2, 16, width), BF16),
        pltpu.VMEM((2, tokens, width), BF16),
        pltpu.VMEM((slices, states, LANES), F32),
        pltpu.VMEM((2, ROWS, inner_width), F32),
        pltpu.VMEM(by_token, F32),
        pltpu.VMEM((2, tokens, state_proj.shape[1]), F32),
        pltpu.VMEM((2 * state_proj.shape[1], tokens), F32),
        pltpu.VMEM(by_token, F32),
        pltpu.VMEM(by_token, BF16),
        pltpu.VMEM((2, tokens * states, inner_width), BF16),
        pltpu.VMEM((2, tokens, 256), BF16),
        pltpu.VMEM(by_token, F32),
        pltpu.VMEM((2, slices, states, tokens, LANES), F32),
        pltpu.VMEM(by_token, F32),
        pltpu.VMEM(by_token, F32),
        pltpu.VMEM(by_token, BF16),
        pltpu.VMEM((GROUP, 3, states, LANES), BF16),
        pltpu.VMEM((GROUP, 3, states, LANES), BF16),
        pltpu.VMEM((2, 2, states, LANES), BF16),
        pltpu.VMEM((FAR, 2, states, LANES), BF16),
        pltpu.VMEM((GROUP, 2, states, LANES), BF16),
        pltpu.VMEM((GROUP, 2, states, LANES), BF16),
        pltpu.VMEM((2, slices, states, LANES), F32),
        pltpu.VMEM((slices, 2, ROWS, LANES), F32),
        pltpu.SemaphoreType.DMA((2,)),
        pltpu.SemaphoreType.DMA((2,)),
        pltpu.SemaphoreType.DMA((GROUP - 1,)),
        pltpu.SemaphoreType.DMA((GROUP - 1,)),
        pltpu.SemaphoreType.DMA((FAR - 1,)),
        pltpu.SemaphoreType.DMA((FAR - 1,)),
        pltpu.SemaphoreType.DMA((GROUP - 1,)),
        pltpu.SemaphoreType.DMA((GROUP - 1,)),
        pltpu.SemaphoreType.DMA((12,)),
        pltpu.SemaphoreType.REGULAR,
    ]
    mixed = pl.pallas_call(
        kernel,
        out_shape=jax.ShapeDtypeStruct((tokens, width), F32),
        in_specs=[hbm] * 11,
        out_specs=vmem,
        scratch_shapes=scratch,
        compiler_params=pltpu.CompilerParams(
            collective_id=0, has_side_effects=True, vmem_limit_bytes=60 << 20
        ),
    )(
        residual_stream,
        norm_gain.reshape(1, -1),
        in_proj,
        conv_weight,
        conv_bias.reshape(1, -1),
        state_proj.T,
        step_proj,
        step_bias.reshape(1, -1),
        decay_rate.T,
        skip_gain.reshape(1, -1),
        out_proj,
    )
    return (residual_stream.astype(F32) + mixed).astype(BF16)


def solution(mesh):
    return jax.shard_map(
        shards,
        mesh=mesh,
        in_specs=(P(("dp", "seq"), None), P(), P(), P(), P(), P(), P(), P(), P(), P(), P()),
        out_specs=P(("dp", "seq"), None),
        check_vma=False,
    )
```

```python
import functools
import math

import jax
import jax.numpy as jnp
from jax import lax
from jax.experimental import pallas as pl
from jax.experimental.pallas import tpu as pltpu
from jax.sharding import PartitionSpec as P

F32 = jnp.float32
BF16 = jnp.bfloat16
LOG2E = math.log2(math.e)
GROUP = 8
FAR = 4
LANES = 128
ROWS = 8
FARTHEST = (4, 3, 5, 2, 6, 1, 7)
SCAN = 40
EARLY = 7


def dot(a, b):
    return jnp.dot(a, b, preferred_element_type=F32)


def dot_nt(a, b):
    return lax.dot_general(a, b, (((1,), (1,)), ((), ())), preferred_element_type=F32)


def split2(v):
    high = v.astype(BF16)
    return high, (v - high.astype(F32)).astype(BF16)


def anti_identity():
    row = lax.broadcasted_iota(jnp.int32, (LANES, LANES), 0)
    col = lax.broadcasted_iota(jnp.int32, (LANES, LANES), 1)
    return (row + col == LANES - 1).astype(F32).astype(BF16)


def flip_lanes(v, anti):
    pieces = [v[:, i : i + LANES] for i in range(0, v.shape[1], LANES)]
    return jnp.concatenate([dot(p, anti) for p in pieces[::-1]], axis=1)


def inv_rms(v):
    return lax.rsqrt(jnp.mean(v * v, axis=-1, keepdims=True) + 1e-05)


def softplus(v):
    return jnp.maximum(v, 0.0) + jnp.log1p(jnp.exp(-jnp.abs(v)))


def silu(v):
    return v * jax.nn.sigmoid(v)


def kernel(
    x_hbm, gain_hbm, in_hbm, cw_hbm, cb_hbm, sp_hbm, tp_hbm, tb_hbm, decay_hbm, skip_hbm, out_hbm,
    o_ref,
    x_ref, gain_ref, in_ref, gate_ref, cw_ref, cb_ref, sp_ref, tp_ref, tb_ref, decay_ref, skip_ref, out_ref,
    halo, nrm, a2, edge, u_s, proj, proj_t, dt_s, du_s, hist, cblk, cum, gc, pre, sg, gmix,
    send_a, recv_a, send_z, recv_z, send_c, recv_c, hin, first_tot, main_gone,
    halo_send, halo_recv, a_send, a_recv, z_send, z_recv, c_send, c_recv, fetched, go,
):
    tokens, width = x_ref.shape
    inner_width = cw_ref.shape[1]
    taps = cw_ref.shape[0]
    rank = tp_ref.shape[0]
    states = decay_ref.shape[0]
    blocks = tokens // ROWS
    slices = inner_width // LANES
    index = lax.axis_index("seq")
    count = GROUP * FAR
    far = index // GROUP
    place = index % GROUP
    left = (index + count - 1) % count
    right = (index + 1) % count
    members = [far * GROUP + (place + d) % GROUP for d in range(1, GROUP)]
    distant = [((far + d) % FAR) * GROUP + place for d in range(1, FAR)]

    barrier = pltpu.get_barrier_semaphore()
    near_z = [distant[0], distant[2]]
    for peer in [left, right] + members + near_z:
        pl.semaphore_signal(
            barrier, inc=1, device_id={"seq": peer}, device_id_type=pl.DeviceIdType.MESH
        )

    def remote(src, dst, send, recv, peer):
        return pltpu.make_async_remote_copy(
            src_ref=src, dst_ref=dst, send_sem=send, recv_sem=recv,
            device_id={"seq": peer}, device_id_type=pl.DeviceIdType.MESH,
        )

    halves = [in_hbm.at[:, pl.ds(i * inner_width, inner_width)] for i in range(2)]
    pairs = [
        (x_hbm, x_ref), (gain_hbm, gain_ref), (halves[0], in_ref), (cw_hbm, cw_ref), (cb_hbm, cb_ref),
        (sp_hbm, sp_ref), (tp_hbm, tp_ref), (tb_hbm, tb_ref), (decay_hbm, decay_ref),
        (halves[1], gate_ref), (skip_hbm, skip_ref), (out_hbm, out_ref),
    ]
    fetches = [pltpu.make_async_copy(src, dst, fetched.at[i]) for i, (src, dst) in enumerate(pairs)]
    for f in fetches[:9]:
        f.start()

    def arrive(first, last):
        for f in fetches[first:last]:
            f.wait()

    arrive(0, 2)

    def a2_wide(first=0, last=slices):
        return jnp.concatenate([a2[k] for k in range(first, last)], axis=1)

    anti = anti_identity()
    gain = gain_ref[...]
    x = x_ref[...]
    x32 = x.astype(F32)
    scale = inv_rms(x32)
    nrm[0] = (x32 * scale * gain).astype(BF16)
    nrm[1] = (flip_lanes(x, anti) * scale * gain).astype(BF16)

    def convolve(v, branch, cols):
        total = cb_ref[:, cols]
        size = v.shape[0]
        for k in range(taps):
            back = taps - 1 - k
            shift = back if branch == 0 else (size - back) % size
            moved = v if back == 0 else pltpu.roll(v, shift, 0)
            total = total + cw_ref[k : k + 1, cols] * moved
        return silu(total).astype(BF16)

    wide = 256
    arrive(2, 9)
    for f in fetches[9:]:
        f.start()
    for k in range(slices):
        a2[k] = decay_ref[:, k * LANES : (k + 1) * LANES] * (-LOG2E)

    def front(i, _):
        cols = pl.ds(pl.multiple_of(i * wide, wide), wide)
        for branch in range(2):
            inner = dot(nrm[branch], in_ref[:, cols])
            edge[branch, :, cols] = inner[:ROWS] if branch == 0 else inner[tokens - ROWS :]
            u_s[branch, :, cols] = convolve(inner, branch, cols).astype(F32)
        return 0

    lax.fori_loop(0, inner_width // wide, front, 0)

    for branch in range(2):
        proj[branch] = dot_nt(u_s[branch].astype(BF16), sp_ref[...])

    def steps(i, _):
        cols = pl.ds(pl.multiple_of(i * wide, wide), wide)
        for branch in range(2):
            low = proj[branch, :, :rank].astype(BF16)
            dt = softplus(dot(low, tp_ref[:, cols]) + tb_ref[:, cols])
            dt_s[branch, :, cols] = dt
            du_s[branch, :, cols] = (dt * u_s[branch, :, cols]).astype(BF16)
        return 0

    lax.fori_loop(0, inner_width // wide, steps, 0)

    pl.semaphore_wait(barrier, 2 + len(members) + len(near_z))
    edge_rows = halo.shape[1]
    to_right = remote(
        x_hbm.at[pl.ds(tokens - edge_rows, edge_rows)], halo.at[0], halo_send.at[0], halo_recv.at[0], right
    )
    to_left = remote(x_hbm.at[pl.ds(0, edge_rows)], halo.at[1], halo_send.at[1], halo_recv.at[1], left)
    to_right.start()
    to_left.start()
    for peer in near_z:
        pl.semaphore_signal(go, inc=1, device_id={"seq": peer}, device_id_type=pl.DeviceIdType.MESH)

    def turn_proj():
        proj_t[...] = jnp.concatenate([proj[0], proj[1]], axis=1).T

    proj_width = proj.shape[2]
    turn_proj()
    half = slices // 2

    lane = lax.broadcasted_iota(jnp.int32, (states, tokens), 1)

    def scan(first, last, size):
        ends = []
        for part in range(2):
            lanes = pl.ds(part * half * LANES, half * LANES)
            rate = a2_wide(part * half, (part + 1) * half)

            def chunk(c, carried, lanes=lanes, rate=rate):
                carried = list(carried)
                base = first * ROWS + c * size
                times = [[base + j, tokens - 1 - base - j] for j in range(size)]
                added = []
                for branch in range(2):
                    top = branch * proj_width + rank
                    maps = proj_t[top : top + states, :]
                    tiles = [jnp.where(lane == t[branch], maps, 0.0).astype(BF16) for t in times]
                    added.append(dot(jnp.concatenate(tiles, axis=0), du_s[branch, :, lanes]))
                for j in range(size):
                    for branch in range(2):
                        t = times[j][branch]
                        dt = jnp.broadcast_to(dt_s[branch, pl.ds(t, 1), lanes], (states, half * LANES))
                        new = added[branch][j * states : (j + 1) * states]
                        h = jnp.exp2(dt * rate) * carried[branch] + new
                        hist[branch, pl.ds(pl.multiple_of(t * states, states), states), lanes] = h.astype(BF16)
                        carried[branch] = h
                return tuple(carried)

            zero = jnp.zeros((states, half * LANES), F32)
            trips = (last - first) * ROWS // size
            ends.append(lax.fori_loop(0, trips, chunk, (zero, zero)))
        return ends

    main = scan(1, blocks, SCAN)
    for part in range(2):
        for branch in range(2):
            for k in range(half):
                hin[branch, part * half + k] = main[part][branch][:, k * LANES : (k + 1) * LANES]

    main_tot = [
        jnp.sum(dt_s[0, ROWS:tokens], axis=0, keepdims=True),
        jnp.sum(dt_s[1, 0 : tokens - ROWS], axis=0, keepdims=True),
    ]
    for branch in range(2):
        for k in range(slices):
            main_gone[branch, k] = jnp.exp2(main_tot[branch][:, k * LANES : (k + 1) * LANES] * a2[k])

    to_right.wait()
    to_left.wait()
    border = halo[...]
    near = border[0, edge_rows - ROWS :].astype(F32)
    far_side = border[1]
    far32 = far_side.astype(F32)
    ahead = near * inv_rms(near) * gain
    behind = (flip_lanes(far_side, anti) * inv_rms(far32) * gain)[:ROWS]
    both = jnp.concatenate([ahead, behind], axis=0).astype(BF16)
    has_left = (index > 0).astype(F32)
    has_right = (index < count - 1).astype(F32)
    border_wide = 512

    def border_front(i, _):
        cols = pl.ds(pl.multiple_of(i * border_wide, border_wide), border_wide)
        v = dot(both, in_ref[:, cols])
        joined = jnp.concatenate([v[:ROWS] * has_left, edge[0, :, cols]], axis=0)
        u_s[0, 0:ROWS, cols] = convolve(joined, 0, cols).astype(F32)[ROWS:]
        joined = jnp.concatenate([edge[1, :, cols], v[ROWS:] * has_right], axis=0)
        u_s[1, tokens - ROWS : tokens, cols] = convolve(joined, 1, cols).astype(F32)[:ROWS]
        return 0

    lax.fori_loop(0, inner_width // border_wide, border_front, 0)
    border_u = jnp.concatenate([u_s[0, 0:ROWS], u_s[1, tokens - ROWS : tokens]], axis=0)
    border_b = border_u.astype(BF16)
    border_p = dot_nt(border_b, sp_ref[...])
    border_maps = dot_nt(sp_ref[rank : rank + states, :], border_b)
    proj[0, 0:ROWS] = border_p[:ROWS]
    proj[1, tokens - ROWS : tokens] = border_p[ROWS:]
    border_dt = softplus(dot(border_p[:, :rank].astype(BF16), tp_ref[...]) + tb_ref[...])
    border_du = (border_dt * border_u).astype(BF16)
    dt_s[0, 0:ROWS] = border_dt[:ROWS]
    dt_s[1, tokens - ROWS : tokens] = border_dt[ROWS:]
    border_lane = lax.broadcasted_iota(jnp.int32, (states, 2 * ROWS), 1)
    start = []
    for branch in range(2):
        spots = [j if branch == 0 else 2 * ROWS - 1 - j for j in range(ROWS)]
        tiles = [jnp.where(border_lane == spot, border_maps, 0.0) for spot in spots]
        new = dot(jnp.concatenate(tiles, axis=0).astype(BF16), border_du)
        h = new[:states]
        for j, spot in enumerate(spots):
            t = spot if branch == 0 else tokens - 2 * ROWS + spot
            if j:
                dt = jnp.broadcast_to(dt_s[branch, t : t + 1, :], (states, inner_width))
                h = jnp.exp2(dt * a2_wide()) * h + new[j * states : (j + 1) * states]
            hist[branch, t * states : (t + 1) * states, :] = h.astype(BF16)
        start.append(h)

    def wide_tile(rows):
        return jnp.concatenate(rows + [jnp.zeros((16 - len(rows), LANES), F32)], axis=0)

    start_tot = [
        jnp.sum(border_dt[:ROWS], axis=0, keepdims=True),
        jnp.sum(border_dt[ROWS:], axis=0, keepdims=True),
    ]

    def tot_rows(values):
        rows = []
        for v in values:
            high = v.astype(BF16).astype(F32)
            rows += [high, v - high]
        return wide_tile(rows).astype(BF16)

    for k in range(slices):
        lanes = slice(k * LANES, (k + 1) * LANES)
        for branch in range(2):
            first = start[branch][:, lanes]
            grown = main_gone[branch, k] * first + hin[branch, k]
            send_a[k, branch] = grown.astype(BF16)
            hin[branch, k] = first
        send_a[k, 2] = tot_rows([(main_tot[b] + start_tot[b])[:, lanes] for b in range(2)])
        for branch in range(2):
            first_tot[k, branch] = jnp.broadcast_to(start_tot[branch][:, lanes], (ROWS, LANES))

    copies_a = []
    for d in FARTHEST:
        target = (place + d) % GROUP
        copies_a.append(
            remote(send_a.at[target], recv_a.at[place], a_send.at[d - 1], a_recv.at[d - 1], members[d - 1])
        )
    for c in copies_a:
        c.start()
    recv_a[place] = send_a[place]
    recv_z[far] = jnp.zeros(recv_z.shape[1:], BF16)

    arrive(9, len(fetches))

    def gates(i, _):
        cols = pl.ds(pl.multiple_of(i * wide, wide), wide)
        for branch in range(2):
            sg[branch, :, cols] = silu(dot(nrm[branch], gate_ref[:, cols]))
        return 0

    lax.fori_loop(0, inner_width // wide, gates, 0)

    t_row = lax.broadcasted_iota(jnp.int32, (tokens, tokens), 0)
    t_col = lax.broadcasted_iota(jnp.int32, (tokens, tokens), 1)
    below = [
        (t_col <= t_row) & ((t_col < ROWS) == (t_row < ROWS)),
        (t_col >= t_row) & ((t_col >= tokens - ROWS) == (t_row >= tokens - ROWS)),
    ]
    for branch in range(2):
        ones = below[branch].astype(F32).astype(BF16)
        high, low = split2(dt_s[branch])
        cum[branch] = dot(ones, high) + dot(ones, low)

    c_first = rank + states
    pick_row = lax.broadcasted_iota(jnp.int32, (states, 256), 0)
    pick_col = lax.broadcasted_iota(jnp.int32, (states, 256), 1)
    spread = (pick_col % states == pick_row).astype(F32).astype(BF16)
    own_row = lax.broadcasted_iota(jnp.int32, (tokens, 256), 0)
    own_col = lax.broadcasted_iota(jnp.int32, (tokens, 256), 1)
    own = own_col // states == own_row % (256 // states)
    for branch in range(2):
        maps = proj[branch, :, c_first : c_first + states].astype(BF16)
        cblk[branch] = jnp.where(own, dot(maps, spread), 0.0).astype(BF16)

    run = 256 // states

    def local_out(i, _):
        rows = pl.ds(pl.multiple_of(i * run, run), run)
        deep = pl.ds(pl.multiple_of(i * 256, 256), 256)
        for branch in range(2):
            local = dot(cblk[branch, rows, :], hist[branch, deep, :])
            pre[branch, rows, :] = local + skip_ref[...] * u_s[branch, rows, :]
        return 0

    lax.fori_loop(0, tokens // run, local_out, 0)

    def factors(i, _):
        rows = pl.ds(pl.multiple_of(i * ROWS, ROWS), ROWS)
        for branch in range(2):
            maps = proj[branch, rows, :]
            for n in range(states):
                c_col = jnp.broadcast_to(maps[:, c_first + n : c_first + n + 1], (ROWS, LANES))
                for k in range(slices):
                    seen = cum[branch, rows, k * LANES : (k + 1) * LANES]
                    gc[branch, k, n, rows, :] = jnp.exp2(seen * a2[k, n : n + 1, :]) * c_col
        return 0

    lax.fori_loop(0, EARLY, factors, 0)

    for c in copies_a:
        c.wait()

    rate = a2[place]
    got_s = [[recv_a[m, b].astype(F32) for m in range(GROUP)] for b in range(2)]
    got_t = []
    for m in range(GROUP):
        rows = recv_a[m, 2].astype(F32)
        got_t.append([rows[0:1] + rows[1:2], rows[2:3] + rows[3:4]])

    prefix = [[None] * GROUP, [None] * GROUP]
    before = [[None] * GROUP, [None] * GROUP]
    for branch in range(2):
        state = jnp.zeros((states, LANES), F32)
        total = jnp.zeros((1, LANES), F32)
        order = range(GROUP) if branch == 0 else range(GROUP - 1, -1, -1)
        for m in order:
            prefix[branch][m] = state
            before[branch][m] = total
            state = jnp.exp2(got_t[m][branch] * rate) * state + got_s[branch][m]
            total = total + got_t[m][branch]
        send_z[branch, 0] = state.astype(BF16)
        send_z[branch, 1] = tot_rows([total])

    pl.semaphore_wait(go, len(near_z))
    copies_z = []
    for d in (1, 0, 2):
        target = (far + d + 1) % FAR
        branch = (target < far).astype(jnp.int32)
        copies_z.append(
            remote(send_z.at[branch], recv_z.at[far], z_send.at[d], z_recv.at[d], distant[d])
        )
    for c in copies_z:
        c.start()

    lax.fori_loop(EARLY, blocks, factors, 0)

    for c in copies_z:
        c.wait()

    for branch in range(2):
        state = jnp.zeros((states, LANES), F32)
        order = range(FAR) if branch == 0 else range(FAR - 1, -1, -1)
        for z in order:
            here = (z < far) if branch == 0 else (z > far)
            rows = recv_z[z, 1].astype(F32)
            later = jnp.exp2((rows[0:1] + rows[1:2]) * rate) * state + recv_z[z, 0].astype(F32)
            state = jnp.where(here, later, state)
        for m in range(GROUP):
            entering = jnp.exp2(before[branch][m] * rate) * state + prefix[branch][m]
            send_c[m, branch] = entering.astype(BF16)

    def back(d):
        target = (place + d) % GROUP
        return remote(
            send_c.at[target], recv_c.at[place], c_send.at[d - 1], c_recv.at[d - 1], far * GROUP + target
        )

    for d in FARTHEST:
        back(d).start()
    recv_c[place] = send_c[place]

    def finish(k):
        cols = pl.ds(pl.multiple_of(k * LANES, LANES), LANES)
        for branch in range(2):
            edge_h = recv_c[k, branch].astype(F32)
            gone = jnp.exp2(first_tot[k, branch, 0:1, :] * a2[k])
            main_h = gone * edge_h + hin[branch, k]
            spread_h = [jnp.broadcast_to(main_h[n : n + 1, :], (ROWS, LANES)) for n in range(states)]
            border_block = 0 if branch == 0 else blocks - 1
            pieces = []
            for b in range(blocks):
                rows = slice(b * ROWS, (b + 1) * ROWS)
                total = pre[branch, rows, cols]
                for n in range(states):
                    if b == border_block:
                        h = jnp.broadcast_to(edge_h[n : n + 1, :], (ROWS, LANES))
                    else:
                        h = spread_h[n]
                    total = total + gc[branch, k, n, rows, :] * h
                pieces.append(total * sg[branch, rows, cols])
                if len(pieces) == 2:
                    gmix[branch, (b - 1) * ROWS : (b + 1) * ROWS, cols] = jnp.concatenate(
                        pieces, axis=0
                    ).astype(BF16)
                    pieces = []

    def finish_next(i, _):
        odd = i % 2
        d = (1 - odd) * (i // 2 + 1) + odd * (GROUP - (i + 1) // 2)
        back(d).wait()
        finish((place + GROUP - d) % GROUP)
        return 0

    finish(place)
    lax.fori_loop(0, GROUP - 1, finish_next, 0)
    forward = dot(gmix[0], out_ref[...]).astype(BF16)
    flipped = flip_lanes(dot(gmix[1], out_ref[...]).astype(BF16), anti)
    o_ref[...] = forward.astype(F32) + flipped


def shards(
    residual_stream, norm_gain, in_proj, conv_weight, conv_bias, state_proj, step_proj,
    step_bias, decay_rate, skip_gain, out_proj,
):
    tokens, width = residual_stream.shape
    inner_width = conv_weight.shape[1]
    states = decay_rate.shape[1]
    rank = step_proj.shape[0]
    columns = state_proj.shape[1]
    slices = inner_width // LANES
    hbm = pl.BlockSpec(memory_space=pl.ANY)
    vmem = pl.BlockSpec(memory_space=pltpu.VMEM)
    by_token = (2, tokens, inner_width)
    scratch = [
        pltpu.VMEM((tokens, width), BF16),
        pltpu.VMEM((1, width), F32),
        pltpu.VMEM((width, inner_width), BF16),
        pltpu.VMEM((width, inner_width), BF16),
        pltpu.VMEM(conv_weight.shape, F32),
        pltpu.VMEM((1, inner_width), F32),
        pltpu.VMEM((columns, inner_width), BF16),
        pltpu.VMEM((rank, inner_width), BF16),
        pltpu.VMEM((1, inner_width), F32),
        pltpu.VMEM((states, inner_width), F32),
        pltpu.VMEM((1, inner_width), F32),
        pltpu.VMEM((inner_width, width), BF16),
        pltpu.VMEM((2, 16, width), BF16),
        pltpu.VMEM((2, tokens, width), BF16),
        pltpu.VMEM((slices, states, LANES), F32),
        pltpu.VMEM((2, ROWS, inner_width), F32),
        pltpu.VMEM(by_token, F32),
        pltpu.VMEM((2, tokens, state_proj.shape[1]), F32),
        pltpu.VMEM((2 * state_proj.shape[1], tokens), F32),
        pltpu.VMEM(by_token, F32),
        pltpu.VMEM(by_token, BF16),
        pltpu.VMEM((2, tokens * states, inner_width), BF16),
        pltpu.VMEM((2, tokens, 256), BF16),
        pltpu.VMEM(by_token, F32),
        pltpu.VMEM((2, slices, states, tokens, LANES), F32),
        pltpu.VMEM(by_token, F32),
        pltpu.VMEM(by_token, F32),
        pltpu.VMEM(by_token, BF16),
        pltpu.VMEM((GROUP, 3, states, LANES), BF16),
        pltpu.VMEM((GROUP, 3, states, LANES), BF16),
        pltpu.VMEM((2, 2, states, LANES), BF16),
        pltpu.VMEM((FAR, 2, states, LANES), BF16),
        pltpu.VMEM((GROUP, 2, states, LANES), BF16),
        pltpu.VMEM((GROUP, 2, states, LANES), BF16),
        pltpu.VMEM((2, slices, states, LANES), F32),
        pltpu.VMEM((slices, 2, ROWS, LANES), F32),
        pltpu.VMEM((2, slices, states, LANES), F32),
        pltpu.SemaphoreType.DMA((2,)),
        pltpu.SemaphoreType.DMA((2,)),
        pltpu.SemaphoreType.DMA((GROUP - 1,)),
        pltpu.SemaphoreType.DMA((GROUP - 1,)),
        pltpu.SemaphoreType.DMA((FAR - 1,)),
        pltpu.SemaphoreType.DMA((FAR - 1,)),
        pltpu.SemaphoreType.DMA((GROUP - 1,)),
        pltpu.SemaphoreType.DMA((GROUP - 1,)),
        pltpu.SemaphoreType.DMA((12,)),
        pltpu.SemaphoreType.REGULAR,
    ]
    mixed = pl.pallas_call(
        kernel,
        out_shape=jax.ShapeDtypeStruct((tokens, width), F32),
        in_specs=[hbm] * 11,
        out_specs=vmem,
        scratch_shapes=scratch,
        compiler_params=pltpu.CompilerParams(
            collective_id=0, has_side_effects=True, vmem_limit_bytes=60 << 20
        ),
    )(
        residual_stream,
        norm_gain.reshape(1, -1),
        in_proj,
        conv_weight,
        conv_bias.reshape(1, -1),
        state_proj.T,
        step_proj,
        step_bias.reshape(1, -1),
        decay_rate.T,
        skip_gain.reshape(1, -1),
        out_proj,
    )
    return (residual_stream.astype(F32) + mixed).astype(BF16)


def solution(mesh):
    return jax.shard_map(
        shards,
        mesh=mesh,
        in_specs=(P(("dp", "seq"), None), P(), P(), P(), P(), P(), P(), P(), P(), P(), P()),
        out_specs=P(("dp", "seq"), None),
        check_vma=False,
    )
```

```python
import functools
import math

import jax
import jax.numpy as jnp
from jax import lax
from jax.experimental import pallas as pl
from jax.experimental.pallas import tpu as pltpu
from jax.sharding import PartitionSpec as P

F32 = jnp.float32
BF16 = jnp.bfloat16
LOG2E = math.log2(math.e)
GROUP = 8
FAR = 4
LANES = 128
ROWS = 8
FARTHEST = (4, 3, 5, 2, 6, 1, 7)
SCAN = 40
EARLY = 4


def dot(a, b):
    return jnp.dot(a, b, preferred_element_type=F32)


def dot_nt(a, b):
    return lax.dot_general(a, b, (((1,), (1,)), ((), ())), preferred_element_type=F32)


def split2(v):
    high = v.astype(BF16)
    return high, (v - high.astype(F32)).astype(BF16)


def anti_identity():
    row = lax.broadcasted_iota(jnp.int32, (LANES, LANES), 0)
    col = lax.broadcasted_iota(jnp.int32, (LANES, LANES), 1)
    return (row + col == LANES - 1).astype(F32).astype(BF16)


def flip_lanes(v, anti):
    pieces = [v[:, i : i + LANES] for i in range(0, v.shape[1], LANES)]
    return jnp.concatenate([dot(p, anti) for p in pieces[::-1]], axis=1)


def inv_rms(v):
    return lax.rsqrt(jnp.mean(v * v, axis=-1, keepdims=True) + 1e-05)


def softplus(v):
    return jnp.maximum(v, 0.0) + jnp.log1p(jnp.exp(-jnp.abs(v)))


def silu(v):
    return v * jax.nn.sigmoid(v)


def kernel(
    x_hbm, gain_hbm, in_hbm, cw_hbm, cb_hbm, sp_hbm, tp_hbm, tb_hbm, decay_hbm, skip_hbm, out_hbm,
    o_ref,
    x_ref, gain_ref, in_ref, gate_ref, cw_ref, cb_ref, sp_ref, tp_ref, tb_ref, decay_ref, skip_ref, out_ref,
    halo, nrm, a2, edge, u_s, proj, proj_t, dt_s, du_s, hist, cblk, cum, gc, pre, sg, added_up,
    send_a, recv_a, send_z, recv_z, send_c, recv_c, hin, first_tot, main_gone,
    halo_send, halo_recv, a_send, a_recv, z_send, z_recv, c_send, c_recv, fetched, go,
):
    tokens, width = x_ref.shape
    inner_width = cw_ref.shape[1]
    taps = cw_ref.shape[0]
    rank = tp_ref.shape[0]
    states = decay_ref.shape[0]
    blocks = tokens // ROWS
    slices = inner_width // LANES
    index = lax.axis_index("seq")
    count = GROUP * FAR
    far = index // GROUP
    place = index % GROUP
    left = (index + count - 1) % count
    right = (index + 1) % count
    members = [far * GROUP + (place + d) % GROUP for d in range(1, GROUP)]
    distant = [((far + d) % FAR) * GROUP + place for d in range(1, FAR)]

    barrier = pltpu.get_barrier_semaphore()
    near_z = [distant[0], distant[2]]
    for peer in [left, right] + members + near_z:
        pl.semaphore_signal(
            barrier, inc=1, device_id={"seq": peer}, device_id_type=pl.DeviceIdType.MESH
        )

    def remote(src, dst, send, recv, peer):
        return pltpu.make_async_remote_copy(
            src_ref=src, dst_ref=dst, send_sem=send, recv_sem=recv,
            device_id={"seq": peer}, device_id_type=pl.DeviceIdType.MESH,
        )

    halves = [in_hbm.at[:, pl.ds(i * inner_width, inner_width)] for i in range(2)]
    pairs = [
        (x_hbm, x_ref), (gain_hbm, gain_ref), (halves[0], in_ref), (cw_hbm, cw_ref), (cb_hbm, cb_ref),
        (sp_hbm, sp_ref), (tp_hbm, tp_ref), (tb_hbm, tb_ref), (decay_hbm, decay_ref),
        (halves[1], gate_ref), (skip_hbm, skip_ref), (out_hbm, out_ref),
    ]
    fetches = [pltpu.make_async_copy(src, dst, fetched.at[i]) for i, (src, dst) in enumerate(pairs)]
    for f in fetches[:9]:
        f.start()

    def arrive(first, last):
        for f in fetches[first:last]:
            f.wait()

    arrive(0, 2)

    def a2_wide(first=0, last=slices):
        return jnp.concatenate([a2[k] for k in range(first, last)], axis=1)

    anti = anti_identity()
    gain = gain_ref[...]
    x = x_ref[...]
    x32 = x.astype(F32)
    scale = inv_rms(x32)
    nrm[0] = (x32 * scale * gain).astype(BF16)
    nrm[1] = (flip_lanes(x, anti) * scale * gain).astype(BF16)

    def convolve(v, branch, cols):
        total = cb_ref[:, cols]
        size = v.shape[0]
        for k in range(taps):
            back = taps - 1 - k
            shift = back if branch == 0 else (size - back) % size
            moved = v if back == 0 else pltpu.roll(v, shift, 0)
            total = total + cw_ref[k : k + 1, cols] * moved
        return silu(total).astype(BF16)

    wide = 256
    arrive(2, 9)
    for f in fetches[9:]:
        f.start()
    for k in range(slices):
        a2[k] = decay_ref[:, k * LANES : (k + 1) * LANES] * (-LOG2E)

    def front(i, _):
        cols = pl.ds(pl.multiple_of(i * wide, wide), wide)
        for branch in range(2):
            inner = dot(nrm[branch], in_ref[:, cols])
            edge[branch, :, cols] = inner[:ROWS] if branch == 0 else inner[tokens - ROWS :]
            u_s[branch, :, cols] = convolve(inner, branch, cols).astype(F32)
        return 0

    lax.fori_loop(0, inner_width // wide, front, 0)

    for branch in range(2):
        proj[branch] = dot_nt(u_s[branch].astype(BF16), sp_ref[...])

    def steps(i, _):
        cols = pl.ds(pl.multiple_of(i * wide, wide), wide)
        for branch in range(2):
            low = proj[branch, :, :rank].astype(BF16)
            dt = softplus(dot(low, tp_ref[:, cols]) + tb_ref[:, cols])
            dt_s[branch, :, cols] = dt
            du_s[branch, :, cols] = (dt * u_s[branch, :, cols]).astype(BF16)
        return 0

    lax.fori_loop(0, inner_width // wide, steps, 0)

    pl.semaphore_wait(barrier, 2 + len(members) + len(near_z))
    edge_rows = halo.shape[1]
    to_right = remote(
        x_hbm.at[pl.ds(tokens - edge_rows, edge_rows)], halo.at[0], halo_send.at[0], halo_recv.at[0], right
    )
    to_left = remote(x_hbm.at[pl.ds(0, edge_rows)], halo.at[1], halo_send.at[1], halo_recv.at[1], left)
    to_right.start()
    to_left.start()
    for peer in near_z:
        pl.semaphore_signal(go, inc=1, device_id={"seq": peer}, device_id_type=pl.DeviceIdType.MESH)

    def turn_proj():
        proj_t[...] = jnp.concatenate([proj[0], proj[1]], axis=1).T

    proj_width = proj.shape[2]
    turn_proj()
    half = slices // 2

    lane = lax.broadcasted_iota(jnp.int32, (states, tokens), 1)

    def scan(first, last, size):
        ends = []
        for part in range(2):
            lanes = pl.ds(part * half * LANES, half * LANES)
            rate = a2_wide(part * half, (part + 1) * half)

            def chunk(c, carried, lanes=lanes, rate=rate):
                carried = list(carried)
                base = first * ROWS + c * size
                times = [[base + j, tokens - 1 - base - j] for j in range(size)]
                added = []
                for branch in range(2):
                    top = branch * proj_width + rank
                    maps = proj_t[top : top + states, :]
                    tiles = [jnp.where(lane == t[branch], maps, 0.0).astype(BF16) for t in times]
                    added.append(dot(jnp.concatenate(tiles, axis=0), du_s[branch, :, lanes]))
                for j in range(size):
                    for branch in range(2):
                        t = times[j][branch]
                        dt = jnp.broadcast_to(dt_s[branch, pl.ds(t, 1), lanes], (states, half * LANES))
                        new = added[branch][j * states : (j + 1) * states]
                        h = jnp.exp2(dt * rate) * carried[branch] + new
                        hist[branch, pl.ds(pl.multiple_of(t * states, states), states), lanes] = h.astype(BF16)
                        carried[branch] = h
                return tuple(carried)

            zero = jnp.zeros((states, half * LANES), F32)
            trips = (last - first) * ROWS // size
            ends.append(lax.fori_loop(0, trips, chunk, (zero, zero)))
        return ends

    main = scan(1, blocks, SCAN)
    for part in range(2):
        for branch in range(2):
            for k in range(half):
                hin[branch, part * half + k] = main[part][branch][:, k * LANES : (k + 1) * LANES]

    main_tot = [
        jnp.sum(dt_s[0, ROWS:tokens], axis=0, keepdims=True),
        jnp.sum(dt_s[1, 0 : tokens - ROWS], axis=0, keepdims=True),
    ]
    for branch in range(2):
        for k in range(slices):
            main_gone[branch, k] = jnp.exp2(main_tot[branch][:, k * LANES : (k + 1) * LANES] * a2[k])

    to_right.wait()
    to_left.wait()
    border = halo[...]
    near = border[0, edge_rows - ROWS :].astype(F32)
    far_side = border[1]
    far32 = far_side.astype(F32)
    ahead = near * inv_rms(near) * gain
    behind = (flip_lanes(far_side, anti) * inv_rms(far32) * gain)[:ROWS]
    both = jnp.concatenate([ahead, behind], axis=0).astype(BF16)
    has_left = (index > 0).astype(F32)
    has_right = (index < count - 1).astype(F32)
    border_wide = 512

    def border_front(i, _):
        cols = pl.ds(pl.multiple_of(i * border_wide, border_wide), border_wide)
        v = dot(both, in_ref[:, cols])
        joined = jnp.concatenate([v[:ROWS] * has_left, edge[0, :, cols]], axis=0)
        u_s[0, 0:ROWS, cols] = convolve(joined, 0, cols).astype(F32)[ROWS:]
        joined = jnp.concatenate([edge[1, :, cols], v[ROWS:] * has_right], axis=0)
        u_s[1, tokens - ROWS : tokens, cols] = convolve(joined, 1, cols).astype(F32)[:ROWS]
        return 0

    lax.fori_loop(0, inner_width // border_wide, border_front, 0)
    border_u = jnp.concatenate([u_s[0, 0:ROWS], u_s[1, tokens - ROWS : tokens]], axis=0)
    border_b = border_u.astype(BF16)
    border_p = dot_nt(border_b, sp_ref[...])
    border_maps = dot_nt(sp_ref[rank : rank + states, :], border_b)
    proj[0, 0:ROWS] = border_p[:ROWS]
    proj[1, tokens - ROWS : tokens] = border_p[ROWS:]
    border_dt = softplus(dot(border_p[:, :rank].astype(BF16), tp_ref[...]) + tb_ref[...])
    border_du = (border_dt * border_u).astype(BF16)
    dt_s[0, 0:ROWS] = border_dt[:ROWS]
    dt_s[1, tokens - ROWS : tokens] = border_dt[ROWS:]
    border_lane = lax.broadcasted_iota(jnp.int32, (states, 2 * ROWS), 1)
    start = []
    for branch in range(2):
        spots = [j if branch == 0 else 2 * ROWS - 1 - j for j in range(ROWS)]
        tiles = [jnp.where(border_lane == spot, border_maps, 0.0) for spot in spots]
        new = dot(jnp.concatenate(tiles, axis=0).astype(BF16), border_du)
        h = new[:states]
        for j, spot in enumerate(spots):
            t = spot if branch == 0 else tokens - 2 * ROWS + spot
            if j:
                dt = jnp.broadcast_to(dt_s[branch, t : t + 1, :], (states, inner_width))
                h = jnp.exp2(dt * a2_wide()) * h + new[j * states : (j + 1) * states]
            hist[branch, t * states : (t + 1) * states, :] = h.astype(BF16)
        start.append(h)

    def wide_tile(rows):
        return jnp.concatenate(rows + [jnp.zeros((16 - len(rows), LANES), F32)], axis=0)

    start_tot = [
        jnp.sum(border_dt[:ROWS], axis=0, keepdims=True),
        jnp.sum(border_dt[ROWS:], axis=0, keepdims=True),
    ]

    def tot_rows(values):
        rows = []
        for v in values:
            high = v.astype(BF16).astype(F32)
            rows += [high, v - high]
        return wide_tile(rows).astype(BF16)

    for k in range(slices):
        lanes = slice(k * LANES, (k + 1) * LANES)
        for branch in range(2):
            first = start[branch][:, lanes]
            grown = main_gone[branch, k] * first + hin[branch, k]
            send_a[k, branch] = grown.astype(BF16)
            hin[branch, k] = first
        send_a[k, 2] = tot_rows([(main_tot[b] + start_tot[b])[:, lanes] for b in range(2)])
        for branch in range(2):
            first_tot[k, branch] = jnp.broadcast_to(start_tot[branch][:, lanes], (ROWS, LANES))

    copies_a = []
    for d in FARTHEST:
        target = (place + d) % GROUP
        copies_a.append(
            remote(send_a.at[target], recv_a.at[place], a_send.at[d - 1], a_recv.at[d - 1], members[d - 1])
        )
    for c in copies_a:
        c.start()
    recv_a[place] = send_a[place]
    recv_z[far] = jnp.zeros(recv_z.shape[1:], BF16)

    arrive(9, len(fetches))

    def gates(i, _):
        cols = pl.ds(pl.multiple_of(i * wide, wide), wide)
        for branch in range(2):
            sg[branch, :, cols] = silu(dot(nrm[branch], gate_ref[:, cols]))
        return 0

    lax.fori_loop(0, inner_width // wide, gates, 0)

    t_row = lax.broadcasted_iota(jnp.int32, (tokens, tokens), 0)
    t_col = lax.broadcasted_iota(jnp.int32, (tokens, tokens), 1)
    below = [
        (t_col <= t_row) & ((t_col < ROWS) == (t_row < ROWS)),
        (t_col >= t_row) & ((t_col >= tokens - ROWS) == (t_row >= tokens - ROWS)),
    ]
    for branch in range(2):
        ones = below[branch].astype(F32).astype(BF16)
        high, low = split2(dt_s[branch])
        cum[branch] = dot(ones, high) + dot(ones, low)

    c_first = rank + states
    pick_row = lax.broadcasted_iota(jnp.int32, (states, 256), 0)
    pick_col = lax.broadcasted_iota(jnp.int32, (states, 256), 1)
    spread = (pick_col % states == pick_row).astype(F32).astype(BF16)
    own_row = lax.broadcasted_iota(jnp.int32, (tokens, 256), 0)
    own_col = lax.broadcasted_iota(jnp.int32, (tokens, 256), 1)
    own = own_col // states == own_row % (256 // states)
    for branch in range(2):
        maps = proj[branch, :, c_first : c_first + states].astype(BF16)
        cblk[branch] = jnp.where(own, dot(maps, spread), 0.0).astype(BF16)

    run = 256 // states

    def local_out(i, _):
        rows = pl.ds(pl.multiple_of(i * run, run), run)
        deep = pl.ds(pl.multiple_of(i * 256, 256), 256)
        for branch in range(2):
            local = dot(cblk[branch, rows, :], hist[branch, deep, :])
            pre[branch, rows, :] = local + skip_ref[...] * u_s[branch, rows, :]
        return 0

    lax.fori_loop(0, tokens // run, local_out, 0)

    def factors(i, _):
        rows = pl.ds(pl.multiple_of(i * ROWS, ROWS), ROWS)
        for branch in range(2):
            maps = proj[branch, rows, :]
            for n in range(states):
                c_col = jnp.broadcast_to(maps[:, c_first + n : c_first + n + 1], (ROWS, LANES))
                for k in range(slices):
                    seen = cum[branch, rows, k * LANES : (k + 1) * LANES]
                    gc[branch, k, n, rows, :] = jnp.exp2(seen * a2[k, n : n + 1, :]) * c_col
        return 0

    lax.fori_loop(0, EARLY, factors, 0)

    for c in copies_a:
        c.wait()

    rate = a2[place]
    got_s = [[recv_a[m, b].astype(F32) for m in range(GROUP)] for b in range(2)]
    got_t = []
    for m in range(GROUP):
        rows = recv_a[m, 2].astype(F32)
        got_t.append([rows[0:1] + rows[1:2], rows[2:3] + rows[3:4]])

    prefix = [[None] * GROUP, [None] * GROUP]
    before = [[None] * GROUP, [None] * GROUP]
    for branch in range(2):
        state = jnp.zeros((states, LANES), F32)
        total = jnp.zeros((1, LANES), F32)
        order = range(GROUP) if branch == 0 else range(GROUP - 1, -1, -1)
        for m in order:
            prefix[branch][m] = state
            before[branch][m] = total
            state = jnp.exp2(got_t[m][branch] * rate) * state + got_s[branch][m]
            total = total + got_t[m][branch]
        send_z[branch, 0] = state.astype(BF16)
        send_z[branch, 1] = tot_rows([total])

    pl.semaphore_wait(go, len(near_z))
    copies_z = []
    for d in (1, 0, 2):
        target = (far + d + 1) % FAR
        branch = (target < far).astype(jnp.int32)
        copies_z.append(
            remote(send_z.at[branch], recv_z.at[far], z_send.at[d], z_recv.at[d], distant[d])
        )
    for c in copies_z:
        c.start()

    lax.fori_loop(EARLY, blocks, factors, 0)

    for c in copies_z:
        c.wait()

    for branch in range(2):
        state = jnp.zeros((states, LANES), F32)
        order = range(FAR) if branch == 0 else range(FAR - 1, -1, -1)
        for z in order:
            here = (z < far) if branch == 0 else (z > far)
            rows = recv_z[z, 1].astype(F32)
            later = jnp.exp2((rows[0:1] + rows[1:2]) * rate) * state + recv_z[z, 0].astype(F32)
            state = jnp.where(here, later, state)
        for m in range(GROUP):
            entering = jnp.exp2(before[branch][m] * rate) * state + prefix[branch][m]
            send_c[m, branch] = entering.astype(BF16)

    def back(d):
        target = (place + d) % GROUP
        return remote(
            send_c.at[target], recv_c.at[place], c_send.at[d - 1], c_recv.at[d - 1], far * GROUP + target
        )

    for d in FARTHEST:
        back(d).start()
    recv_c[place] = send_c[place]

    def finish(k):
        cols = pl.ds(pl.multiple_of(k * LANES, LANES), LANES)
        both = []
        for branch in range(2):
            mixes = []
            edge_h = recv_c[k, branch].astype(F32)
            gone = jnp.exp2(first_tot[k, branch, 0:1, :] * a2[k])
            main_h = gone * edge_h + hin[branch, k]
            spread_h = [jnp.broadcast_to(main_h[n : n + 1, :], (ROWS, LANES)) for n in range(states)]
            border_block = 0 if branch == 0 else blocks - 1
            pieces = []
            for b in range(blocks):
                rows = slice(b * ROWS, (b + 1) * ROWS)
                total = pre[branch, rows, cols]
                for n in range(states):
                    if b == border_block:
                        h = jnp.broadcast_to(edge_h[n : n + 1, :], (ROWS, LANES))
                    else:
                        h = spread_h[n]
                    total = total + gc[branch, k, n, rows, :] * h
                pieces.append(total * sg[branch, rows, cols])
                if len(pieces) == 2:
                    mixes.append(jnp.concatenate(pieces, axis=0).astype(BF16))
                    pieces = []
            both.append(jnp.concatenate(mixes, axis=0))
        return both, out_ref[cols, :]

    def add_up(one, other, first=False):
        weights = jnp.concatenate([one[1], other[1]], axis=0)
        for branch in range(2):
            share = dot(jnp.concatenate([one[0][branch], other[0][branch]], axis=1), weights)
            added_up[branch] = share if first else added_up[branch] + share

    def arrived(d):
        back(d).wait()
        return finish((place + GROUP - d) % GROUP)

    def finish_pair(i, _):
        one = arrived(GROUP - 1 - i)
        add_up(one, arrived(2 + i))
        return 0

    own = finish(place)
    add_up(own, arrived(1), True)
    lax.fori_loop(0, GROUP // 2 - 1, finish_pair, 0)
    forward = added_up[0].astype(BF16)
    flipped = flip_lanes(added_up[1].astype(BF16), anti)
    o_ref[...] = forward.astype(F32) + flipped


def shards(
    residual_stream, norm_gain, in_proj, conv_weight, conv_bias, state_proj, step_proj,
    step_bias, decay_rate, skip_gain, out_proj,
):
    tokens, width = residual_stream.shape
    inner_width = conv_weight.shape[1]
    states = decay_rate.shape[1]
    rank = step_proj.shape[0]
    columns = state_proj.shape[1]
    slices = inner_width // LANES
    hbm = pl.BlockSpec(memory_space=pl.ANY)
    vmem = pl.BlockSpec(memory_space=pltpu.VMEM)
    by_token = (2, tokens, inner_width)
    scratch = [
        pltpu.VMEM((tokens, width), BF16),
        pltpu.VMEM((1, width), F32),
        pltpu.VMEM((width, inner_width), BF16),
        pltpu.VMEM((width, inner_width), BF16),
        pltpu.VMEM(conv_weight.shape, F32),
        pltpu.VMEM((1, inner_width), F32),
        pltpu.VMEM((columns, inner_width), BF16),
        pltpu.VMEM((rank, inner_width), BF16),
        pltpu.VMEM((1, inner_width), F32),
        pltpu.VMEM((states, inner_width), F32),
        pltpu.VMEM((1, inner_width), F32),
        pltpu.VMEM((inner_width, width), BF16),
        pltpu.VMEM((2, 16, width), BF16),
        pltpu.VMEM((2, tokens, width), BF16),
        pltpu.VMEM((slices, states, LANES), F32),
        pltpu.VMEM((2, ROWS, inner_width), F32),
        pltpu.VMEM(by_token, F32),
        pltpu.VMEM((2, tokens, state_proj.shape[1]), F32),
        pltpu.VMEM((2 * state_proj.shape[1], tokens), F32),
        pltpu.VMEM(by_token, F32),
        pltpu.VMEM(by_token, BF16),
        pltpu.VMEM((2, tokens * states, inner_width), BF16),
        pltpu.VMEM((2, tokens, 256), BF16),
        pltpu.VMEM(by_token, F32),
        pltpu.VMEM((2, slices, states, tokens, LANES), F32),
        pltpu.VMEM(by_token, F32),
        pltpu.VMEM(by_token, F32),
        pltpu.VMEM((2, tokens, width), F32),
        pltpu.VMEM((GROUP, 3, states, LANES), BF16),
        pltpu.VMEM((GROUP, 3, states, LANES), BF16),
        pltpu.VMEM((2, 2, states, LANES), BF16),
        pltpu.VMEM((FAR, 2, states, LANES), BF16),
        pltpu.VMEM((GROUP, 2, states, LANES), BF16),
        pltpu.VMEM((GROUP, 2, states, LANES), BF16),
        pltpu.VMEM((2, slices, states, LANES), F32),
        pltpu.VMEM((slices, 2, ROWS, LANES), F32),
        pltpu.VMEM((2, slices, states, LANES), F32),
        pltpu.SemaphoreType.DMA((2,)),
        pltpu.SemaphoreType.DMA((2,)),
        pltpu.SemaphoreType.DMA((GROUP - 1,)),
        pltpu.SemaphoreType.DMA((GROUP - 1,)),
        pltpu.SemaphoreType.DMA((FAR - 1,)),
        pltpu.SemaphoreType.DMA((FAR - 1,)),
        pltpu.SemaphoreType.DMA((GROUP - 1,)),
        pltpu.SemaphoreType.DMA((GROUP - 1,)),
        pltpu.SemaphoreType.DMA((12,)),
        pltpu.SemaphoreType.REGULAR,
    ]
    mixed = pl.pallas_call(
        kernel,
        out_shape=jax.ShapeDtypeStruct((tokens, width), F32),
        in_specs=[hbm] * 11,
        out_specs=vmem,
        scratch_shapes=scratch,
        compiler_params=pltpu.CompilerParams(
            collective_id=0, has_side_effects=True, vmem_limit_bytes=60 << 20
        ),
    )(
        residual_stream,
        norm_gain.reshape(1, -1),
        in_proj,
        conv_weight,
        conv_bias.reshape(1, -1),
        state_proj.T,
        step_proj,
        step_bias.reshape(1, -1),
        decay_rate.T,
        skip_gain.reshape(1, -1),
        out_proj,
    )
    return (residual_stream.astype(F32) + mixed).astype(BF16)


def solution(mesh):
    return jax.shard_map(
        shards,
        mesh=mesh,
        in_specs=(P(("dp", "seq"), None), P(), P(), P(), P(), P(), P(), P(), P(), P(), P()),
        out_specs=P(("dp", "seq"), None),
        check_vma=False,
    )
```
